32 devices in a mesh: dp: 8 (over y, x, core), seq: 4 (over z).
Axes of the slice: x: 2, y: 2, z: 4, core: 2. Of those that a mesh axis runs over, the one named last changes fastest.
Arguments:
- hidden: bfloat16 [8192, 1792], P(('dp', 'seq')), may hold values from -12.75 to 12.75
- depths: int32 [8192], P(('dp', 'seq')), may hold values from 1 to 3, as said below
- packed_slot_index: int32 [8192], P(('dp', 'seq')), may hold values from -1 to 511, as said below
- value_weight: bfloat16 [1792, 1024], P('dp'), may hold values from -0.125 to 0.125
- output_weight: bfloat16 [1024, 1792], P('dp'), may hold values from -0.1875 to 0.1875
- adapter_down_factor: bfloat16 [1792, 128], P('dp'), may hold values from -0.125 to 0.125
- adapter_up_factor: bfloat16 [1024, 128], P('dp'), may hold values from -0.5 to 0.5
- before_norm_gain: float32 [1792], replicated, may hold values from 0.1 to 1.9
- after_norm_gain: float32 [1792], replicated, may hold values from 0.1 to 1.9
- cotangent: bfloat16 [4096, 1792], P(('dp', 'seq')), may hold values from -6 to 6
Outputs:
- looped: bfloat16 [4096, 1792], P(('dp', 'seq'))
- grad_hidden: bfloat16 [8192, 1792], P(('dp', 'seq'))
- down_factor_gradient: float32 [1792, 128], P('dp', 'seq')
- up_factor_gradient: float32 [1024, 128], P('dp', 'seq')
The draws below stay inside these ranges and needn't reach their ends.
Inputs may be any that keep to these rules, and one draw needn't show every extreme that they name: `depths`: of the 1024 tokens of one dp index exactly 512 have depth 2 or 3, and all 256 tokens of one seq index are among them. -1 exactly where depths is 1. Over the tokens of one dp index with depth 2 or 3 the slots are a permutation of 0 to 511; packed_slot_index // 128 is the seq index that holds the token's packed row. At most 64 tokens of one device have slots of one seq index, and exactly 64 do in every dp index.
All inputs are finite; a program needn't handle non-finite values.
Results may differ from the reference program's by a relative error of at most 0.01.
Values may be sent and summed in bfloat16 or wider, within the bound.
A program may use at most 64 MiB of HBM per device.

```python
import math
import jax
import jax.numpy as jnp
from jax import lax

MODEL_WIDTH = 1792
VALUE_WIDTH = 1024
LOW_RANK_SIZE = 128
TOK_DEV = 256
GROUP_TOKENS = 1024
TOKENS = 8192
ACT_DEV = 128
GROUP_ROWS = 512
ALL_ACTIVE = 4096


def routing(key):
    base_key = jax.random.fold_in(key, 7)
    key_busy, key_pick, key_place, key_deep, key_turn = jax.random.split(base_key, 5)
    seq_count = GROUP_TOKENS // TOK_DEV
    groups = TOKENS // GROUP_TOKENS
    busy_dev = jax.random.randint(key_busy, (groups,), 0, seq_count)
    other_rows = (seq_count - 1) * TOK_DEV
    needed = GROUP_ROWS - TOK_DEV
    shuffled = jax.vmap(lambda one_key: jax.random.permutation(one_key, other_rows))(jax.random.split(key_pick, groups))
    chosen = (shuffled < needed).reshape(groups, seq_count - 1, TOK_DEV)
    device_ids = jnp.arange(seq_count, dtype=jnp.int32)[None, :]
    is_busy = device_ids == busy_dev[:, None]
    other_rank = jnp.clip(device_ids - (device_ids > busy_dev[:, None]).astype(jnp.int32), 0, seq_count - 2)
    picked = jnp.take_along_axis(chosen, jnp.broadcast_to(other_rank[:, :, None], (groups, seq_count, TOK_DEV)), axis=1)
    active = jnp.where(is_busy[:, :, None], True, picked).reshape(groups, GROUP_TOKENS)
    active_int = active.astype(jnp.int32)
    order_in = jnp.cumsum(active_int, axis=1) - active_int
    turn = jax.random.randint(key_turn, (groups, 1), 0, seq_count)
    dest_dev = (order_in + turn) % seq_count
    window = jnp.minimum(order_in // seq_count, ACT_DEV - 1)
    placing = jax.vmap(lambda one_key: jax.random.permutation(one_key, ACT_DEV))(jax.random.split(key_place, groups * seq_count))
    flat_place = placing.reshape(groups, seq_count * ACT_DEV).astype(jnp.int32)
    dest_pos = jnp.take_along_axis(flat_place, dest_dev * ACT_DEV + window, axis=1)
    slots = jnp.where(active, dest_dev * ACT_DEV + dest_pos, -1)
    deeper = jax.random.randint(key_deep, (groups, GROUP_TOKENS), 2, 4)
    depth_draw = jnp.where(active, deeper, 1)
    return (depth_draw.reshape(TOKENS).astype(jnp.int32), slots.reshape(TOKENS).astype(jnp.int32))


def draw_depths(key, part):
    return routing(key)[0]


def draw_packed_slot_index(key, part):
    return routing(key)[1]


def draw_hidden(key, part):
    key_base, key_rows, key_cols = jax.random.split(jax.random.fold_in(key, 11), 3)
    row_scale = jnp.exp(jax.random.uniform(key_rows, (TOKENS, 1), jnp.float32, math.log(0.6), math.log(1.7)))
    col_scale = jnp.exp(jax.random.uniform(key_cols, (1, MODEL_WIDTH), jnp.float32, math.log(0.4), math.log(2.5)))
    base_draw = jax.random.truncated_normal(key_base, -3.0, 3.0, (TOKENS, MODEL_WIDTH), jnp.float32)
    return (base_draw * row_scale * col_scale).astype(jnp.bfloat16)


def steps_of(own_key, extent, cuts, low, largest):
    level, own = 1.0, jax.random.fold_in(own_key, 6)
    for axis_at, blocks in cuts:
        draws = jnp.exp(jax.random.uniform(jax.random.fold_in(own, axis_at), (blocks,), jnp.float32, low / len(cuts), largest / len(cuts)))
        level = level * jnp.repeat(draws, extent[axis_at] // blocks).reshape([-1 if axis == axis_at else 1 for axis in range(len(extent))])
    return level


def centred(own_key, extent, spread, most, shards=(), kind=jnp.bfloat16):
    gain = steps_of(own_key, extent, shards, -0.22, 0.18) if shards else 1.0
    result = jax.random.normal(own_key, extent, jnp.float32) * spread * gain
    return jnp.minimum(jnp.maximum(result, -most), most).astype(kind)


def setup_inputs(seed: int = 0) -> dict:
    splits = jax.random.split(jax.random.key(seed), 11)
    return {
        "hidden": draw_hidden(jax.random.fold_in(splits[10], 71), 0),
        "depths": draw_depths(jax.random.fold_in(splits[10], 71), 0),
        "packed_slot_index": draw_packed_slot_index(jax.random.fold_in(splits[10], 71), 0),
        "value_weight": centred(splits[3], (MODEL_WIDTH, VALUE_WIDTH), MODEL_WIDTH ** -0.5, 0.125, ((0, 8),)),
        "output_weight": centred(splits[4], (VALUE_WIDTH, MODEL_WIDTH), VALUE_WIDTH ** -0.5, 0.1875, ((0, 8),)),
        "adapter_down_factor": centred(splits[5], (MODEL_WIDTH, LOW_RANK_SIZE), MODEL_WIDTH ** -0.5, 0.125, ((0, 8),)),
        "adapter_up_factor": centred(splits[6], (VALUE_WIDTH, LOW_RANK_SIZE), LOW_RANK_SIZE ** -0.5, 0.5, ((0, 8),)),
        "before_norm_gain": jnp.clip(1.0 + 0.18 * jax.random.normal(splits[7], (MODEL_WIDTH,), jnp.float32), 0.1, 1.9),
        "after_norm_gain": jnp.clip(1.0 + 0.18 * jax.random.normal(splits[8], (MODEL_WIDTH,), jnp.float32), 0.1, 1.9),
        "cotangent": centred(splits[9], (ALL_ACTIVE, MODEL_WIDTH), 1.0, 6.0, ((0, 32),)),
    }


epsilon = 1e-06

def contract_final_axis(left, right):
    return lax.dot_general(left, right, (((1,), (1,)), ((), ())), preferred_element_type=jnp.float32)

def contract_first(left, right):
    return lax.dot_general(left, right, (((0,), (0,)), ((), ())), preferred_element_type=jnp.float32)

def layer_forward(input_rows, cotangent_rows, value_weight, output_weight, adapter_down_factor, adapter_up_factor, before_norm_gain, after_norm_gain):
    x_float = input_rows.astype(jnp.float32)
    inv_pre = lax.rsqrt(lax.optimization_barrier(jnp.mean(x_float * x_float, axis=-1, keepdims=True)) + epsilon)
    whitened = x_float * inv_pre
    normalized_rows = (whitened * before_norm_gain).astype(jnp.bfloat16)
    rank_reduced = jnp.dot(normalized_rows, adapter_down_factor, preferred_element_type=jnp.float32).astype(jnp.bfloat16)
    projected_rows = (jnp.dot(normalized_rows, value_weight, preferred_element_type=jnp.float32) + contract_final_axis(rank_reduced, adapter_up_factor)).astype(jnp.bfloat16)
    mixed_out = jnp.dot(projected_rows, output_weight, preferred_element_type=jnp.float32)
    inv_post = lax.rsqrt(lax.optimization_barrier(jnp.mean(mixed_out * mixed_out, axis=-1, keepdims=True)) + epsilon)
    shaped = mixed_out * inv_post
    looped = (x_float + shaped * after_norm_gain).astype(jnp.bfloat16)
    cot_float = cotangent_rows.astype(jnp.float32)
    grad_shaped = cot_float * after_norm_gain
    grad_mixed = (inv_post * (grad_shaped - shaped * lax.optimization_barrier(jnp.mean(grad_shaped * shaped, axis=-1, keepdims=True)))).astype(jnp.bfloat16)
    value_gradient = contract_final_axis(grad_mixed, output_weight).astype(jnp.bfloat16)
    low_rank_gradient = jnp.dot(value_gradient, adapter_up_factor, preferred_element_type=jnp.float32).astype(jnp.bfloat16)
    normalized_gradient = contract_final_axis(value_gradient, value_weight) + contract_final_axis(low_rank_gradient, adapter_down_factor)
    grad_white = normalized_gradient * before_norm_gain
    gradient_rows = (cot_float + inv_pre * (grad_white - whitened * lax.optimization_barrier(jnp.mean(grad_white * whitened, axis=-1, keepdims=True)))).astype(jnp.bfloat16)
    down_factor_gradient = contract_first(normalized_rows, low_rank_gradient)
    up_factor_gradient = contract_first(value_gradient, rank_reduced)
    return (looped, gradient_rows, down_factor_gradient, up_factor_gradient)

def reference(hidden, depths, packed_slot_index, value_weight, output_weight, adapter_down_factor, adapter_up_factor, before_norm_gain, after_norm_gain, cotangent):
    active = depths >= 2
    group_of = jnp.arange(TOKENS, dtype=jnp.int32) // GROUP_TOKENS
    target = jnp.where(active, group_of * GROUP_ROWS + packed_slot_index, ALL_ACTIVE).astype(jnp.int32)
    packed = jnp.zeros((ALL_ACTIVE, MODEL_WIDTH), jnp.bfloat16).at[target].set(hidden, mode='drop')
    groups = ALL_ACTIVE // GROUP_ROWS

    def step_fn(totals, pieces):
        entering_rows, incoming_cotangent = pieces
        looped, gradient_rows, down_factor_gradient, up_factor_gradient = layer_forward(entering_rows, incoming_cotangent, value_weight, output_weight, adapter_down_factor, adapter_up_factor, before_norm_gain, after_norm_gain)
        return ((totals[0] + down_factor_gradient, totals[1] + up_factor_gradient), (looped, gradient_rows))
    init = (jnp.zeros((MODEL_WIDTH, LOW_RANK_SIZE), jnp.float32), jnp.zeros((VALUE_WIDTH, LOW_RANK_SIZE), jnp.float32))
    totals, outputs = lax.scan(step_fn, init, (packed.reshape(groups, GROUP_ROWS, MODEL_WIDTH), cotangent.reshape(groups, GROUP_ROWS, MODEL_WIDTH)))
    looped = outputs[0].reshape(ALL_ACTIVE, MODEL_WIDTH)
    gradient_rows = outputs[1].reshape(ALL_ACTIVE, MODEL_WIDTH)
    picked = jnp.take(gradient_rows, jnp.minimum(target, ALL_ACTIVE - 1), axis=0)
    grad_hidden = jnp.where(active[:, None], picked, jnp.zeros((), jnp.bfloat16))
    grad_scale = 1.0 / math.sqrt(ALL_ACTIVE)
    return (looped, grad_hidden, totals[0] * grad_scale, totals[1] * grad_scale)
```

```python
import functools
import math

import jax
import jax.numpy as jnp
from jax import lax
from jax.experimental import pallas as pl
from jax.experimental.pallas import tpu as pltpu
from jax.sharding import PartitionSpec as P

epsilon = 1e-06


def contract_final_axis(left, right):
    return lax.dot_general(
        left, right, (((1,), (1,)), ((), ())), preferred_element_type=jnp.float32
    )


def contract_first(left, right):
    return lax.dot_general(
        left, right, (((0,), (0,)), ((), ())), preferred_element_type=jnp.float32
    )


def layer_forward(
    input_rows,
    cotangent_rows,
    value_weight,
    output_weight,
    adapter_down_factor,
    adapter_up_factor,
    before_norm_gain,
    after_norm_gain,
):
    x_float = input_rows.astype(jnp.float32)
    inv_pre = lax.rsqrt(jnp.mean(x_float * x_float, axis=-1, keepdims=True) + epsilon)
    whitened = x_float * inv_pre
    normalized_rows = (whitened * before_norm_gain).astype(jnp.bfloat16)
    rank_reduced = jnp.dot(
        normalized_rows, adapter_down_factor, preferred_element_type=jnp.float32
    ).astype(jnp.bfloat16)
    projected_rows = (
        jnp.dot(normalized_rows, value_weight, preferred_element_type=jnp.float32)
        + contract_final_axis(rank_reduced, adapter_up_factor)
    ).astype(jnp.bfloat16)
    mixed_out = jnp.dot(projected_rows, output_weight, preferred_element_type=jnp.float32)
    inv_post = lax.rsqrt(jnp.mean(mixed_out * mixed_out, axis=-1, keepdims=True) + epsilon)
    shaped = mixed_out * inv_post
    looped = (x_float + shaped * after_norm_gain).astype(jnp.bfloat16)
    cot_float = cotangent_rows.astype(jnp.float32)
    grad_shaped = cot_float * after_norm_gain
    grad_mixed = (
        inv_post * (grad_shaped - shaped * jnp.mean(grad_shaped * shaped, axis=-1, keepdims=True))
    ).astype(jnp.bfloat16)
    value_gradient = contract_final_axis(grad_mixed, output_weight).astype(jnp.bfloat16)
    low_rank_gradient = jnp.dot(
        value_gradient, adapter_up_factor, preferred_element_type=jnp.float32
    ).astype(jnp.bfloat16)
    normalized_gradient = contract_final_axis(value_gradient, value_weight) + contract_final_axis(
        low_rank_gradient, adapter_down_factor
    )
    grad_white = normalized_gradient * before_norm_gain
    gradient_rows = (
        cot_float
        + inv_pre
        * (grad_white - whitened * jnp.mean(grad_white * whitened, axis=-1, keepdims=True))
    ).astype(jnp.bfloat16)
    down_factor_gradient = contract_first(normalized_rows, low_rank_gradient)
    up_factor_gradient = contract_first(value_gradient, rank_reduced)
    return (looped, gradient_rows, down_factor_gradient, up_factor_gradient)


def general_body(
    hidden,
    depths,
    packed_slot_index,
    value_weight,
    output_weight,
    adapter_down_factor,
    adapter_up_factor,
    before_norm_gain,
    after_norm_gain,
    cotangent,
):
    seq_count = lax.axis_size("seq")
    own_index = lax.axis_index("seq")
    tok_count = hidden.shape[0]
    act_rows = cotangent.shape[0]
    value_full, out_full, down_full, up_full = (
        lax.all_gather(value_weight, "dp", axis=0, tiled=True),
        lax.all_gather(output_weight, "dp", axis=0, tiled=True),
        lax.all_gather(adapter_down_factor, "dp", axis=0, tiled=True),
        lax.all_gather(adapter_up_factor, "dp", axis=0, tiled=True),
    )
    depth_all, slot_all = (
        lax.all_gather(depths, "seq", axis=0, tiled=True),
        lax.all_gather(packed_slot_index, "seq", axis=0, tiled=True),
    )
    active_all = depth_all >= 2
    dest_all = jnp.where(active_all, slot_all // act_rows, -1)
    pos_all = jnp.where(active_all, slot_all % act_rows, 0)
    mine = active_all & (dest_all == own_index)
    active = depths >= 2
    zero_row = jnp.zeros((), jnp.bfloat16)
    rows_all = lax.all_gather(hidden, "seq", axis=0, tiled=True)
    source = (
        jnp.zeros((act_rows,), jnp.int32)
        .at[jnp.where(mine, pos_all, act_rows)]
        .set(jnp.arange(seq_count * tok_count, dtype=jnp.int32), mode="drop")
    )
    packed = jnp.take(rows_all, source, axis=0)
    looped, gradient_rows, down_factor_gradient, up_factor_gradient = layer_forward(
        packed,
        cotangent,
        value_full,
        out_full,
        down_full,
        up_full,
        before_norm_gain,
        after_norm_gain,
    )
    grads_all = lax.all_gather(gradient_rows, "seq", axis=0, tiled=True)
    picked = jnp.take(grads_all, jnp.maximum(packed_slot_index, 0), axis=0)
    grad_hidden = jnp.where(active[:, None], picked, zero_row)
    grad_scale = 1.0 / math.sqrt(seq_count * act_rows * lax.axis_size("dp"))
    down_term = down_factor_gradient * grad_scale
    up_term = up_factor_gradient * grad_scale
    down_mid, up_mid = (
        lax.psum_scatter(
            down_term.astype(jnp.bfloat16), "seq", scatter_dimension=1, tiled=True
        ).astype(jnp.float32),
        lax.psum_scatter(
            up_term.astype(jnp.bfloat16), "seq", scatter_dimension=1, tiled=True
        ).astype(jnp.float32),
    )
    down_sum, up_sum = (
        lax.psum_scatter(down_mid, "dp", scatter_dimension=0, tiled=True),
        lax.psum_scatter(up_mid, "dp", scatter_dimension=0, tiled=True),
    )
    return (looped, grad_hidden, down_sum, up_sum)


MESH = pl.DeviceIdType.MESH
BF, F32 = jnp.bfloat16, jnp.float32
CAP = 64


def dot(left, right, left_axis=1, right_axis=0):
    return lax.dot_general(
        left, right, (((left_axis,), (right_axis,)), ((), ())), preferred_element_type=F32
    )


def fused_kernel(
    slot_ref, depth_ref, gain_b_ref, gain_a_ref, hidden_hbm, cot_hbm, wv_in, wo_in, dn_in, up_in,
    looped_hbm, gh_hbm, down_out, up_out,
    wv, wo, dn, up, hid, cot, sendb, recvb, gsend, grecv, lsend, lrecv, zsend, zrecv,
    place, unplace, normed, low, proj, mixed, gv, gn, packed, looped,
    w_send, w_recv, s_send, s_recv, l_send, l_recv, g_send, g_recv, z_send, z_recv, loc,
):
    dp, seq = lax.axis_index("dp"), lax.axis_index("seq")
    n_dp, n_seq = 8, 4
    width = hid.shape[1]
    core, x, y = dp % 2, (dp // 2) % 2, dp // 4
    nbr_x, nbr_y, sib = dp + 2 - 4 * x, dp + 4 - 8 * y, dp + 1 - 2 * core
    diag = nbr_x + 4 - 8 * y
    to_sib = 1 - 2 * core

    local = [
        pltpu.make_async_copy(hidden_hbm, hid, loc.at[0]),
        pltpu.make_async_copy(cot_hbm, cot, loc.at[1]),
    ]
    arrays = [(dn_in, dn), (up_in, up), (wv_in, wv), (wo_in, wo)]
    for number, (shard, full) in enumerate(arrays):
        rows = shard.shape[0]
        local.append(
            pltpu.make_async_copy(
                shard, full.at[pl.ds(pl.multiple_of(dp * rows, 16), rows), :], loc.at[2 + number]
            )
        )
    for copy in local:
        copy.start()

    barrier = pltpu.get_barrier_semaphore()
    for k in range(1, n_dp):
        pl.semaphore_signal(barrier, inc=1, device_id=((dp + k) % n_dp, seq), device_id_type=MESH)
    for k in range(1, n_seq):
        pl.semaphore_signal(barrier, inc=1, device_id=(dp, (seq + k) % n_seq), device_id_type=MESH)

    tok = hid.shape[0]
    slots = slot_ref[...]
    act = depth_ref[...] >= 2
    dest = jnp.where(act, slots // 128, -1)
    where_to = lax.broadcasted_iota(jnp.int32, (8, tok), 0) == dest
    earlier = (
        lax.broadcasted_iota(jnp.int32, (tok, tok), 0)
        < lax.broadcasted_iota(jnp.int32, (tok, tok), 1)
    ).astype(F32).astype(BF)
    counts = dot(where_to.astype(F32).astype(BF), earlier)
    rank = jnp.sum(jnp.where(where_to, counts, 0.0), axis=0, keepdims=True)
    row_of = jnp.where(act, dest.astype(F32) * CAP + rank, -1.0)
    picked = (lax.broadcasted_iota(jnp.int32, (n_seq * CAP, tok), 0).astype(F32) == row_of).astype(F32)
    place[...] = picked.astype(BF)
    position = jnp.where(act, slots - dest * 128 + 1, 0).astype(F32)
    pos_col = jnp.sum(picked * position, axis=1, keepdims=True) - 1.0
    sendb[:, width:] = jnp.broadcast_to(pos_col, (n_seq * CAP, 128)).astype(BF)

    pl.semaphore_wait(barrier, n_dp - 1 + n_seq - 1)

    def region(a, owner, half):
        shard, full = arrays[a]
        rows = shard.shape[0]
        if half is None:
            return full.at[pl.ds(pl.multiple_of(owner * rows, 16), rows), :]
        part = rows // 2
        return full.at[pl.ds(pl.multiple_of(owner * rows + half * part, 16), part), :]

    def piece(a, number, owner, half, target, from_input=False):
        dst = region(a, owner, half)
        if from_input:
            shard = arrays[a][0]
            part = shard.shape[0] // 2
            source = shard if half is None else shard.at[pl.ds(half * part, part), :]
        else:
            source = dst
        return pltpu.make_async_remote_copy(
            src_ref=source, dst_ref=dst, send_sem=w_send.at[a * 13 + number],
            recv_sem=w_recv.at[a * 13 + number], device_id=(target, seq), device_id_type=MESH,
        )

    pending = []

    def send(*args, **kw):
        copy = piece(*args, **kw)
        copy.start()
        pending.append(copy)

    def got(a, number, owner, half):
        piece(a, number, owner, half, sib).wait_recv()

    def own(a):
        send(a, 0, dp, 0, nbr_x, from_input=True)
        send(a, 3, dp, 1, nbr_y, from_input=True)
        send(a, 1, dp, 1, nbr_x, from_input=True)
        send(a, 2, dp, 0, nbr_y, from_input=True)
        send(a, 6, dp, None, sib, from_input=True)

    def forward_first(a):
        got(a, 0, nbr_x, 0)
        send(a, 4, nbr_x, 0, nbr_y)
        send(a, 7, nbr_x, 0, sib)
        got(a, 3, nbr_y, 1)
        send(a, 5, nbr_y, 1, nbr_x)
        send(a, 8, nbr_y, 1, sib)

    def forward_second(a):
        got(a, 1, nbr_x, 1)
        send(a, 9, nbr_x, 1, sib)
        got(a, 2, nbr_y, 0)
        send(a, 10, nbr_y, 0, sib)

    def forward_diag(a):
        got(a, 4, diag, 0)
        send(a, 11, diag, 0, sib)
        got(a, 5, diag, 1)
        send(a, 12, diag, 1, sib)

    def finish(a):
        got(a, 6, sib, None)
        got(a, 7, nbr_x + to_sib, 0)
        got(a, 8, nbr_y + to_sib, 1)
        got(a, 9, nbr_x + to_sib, 1)
        got(a, 10, nbr_y + to_sib, 0)
        got(a, 11, diag + to_sib, 0)
        got(a, 12, diag + to_sib, 1)

    for a in (0, 1, 2):
        own(a)

    def block(owner, rows):
        return pl.ds(pl.multiple_of(owner * rows, 16), rows)

    def exchange(src_buf, dst_buf, sends, recvs, k):
        target = (seq + k) % n_seq
        return pltpu.make_async_remote_copy(
            src_ref=src_buf.at[block(target, CAP), :], dst_ref=dst_buf.at[block(seq, CAP), :],
            send_sem=sends.at[k], recv_sem=recvs.at[k], device_id=(dp, target), device_id_type=MESH,
        )

    def arrival(src_buf, dst_buf, sends, recvs, k):
        origin = (seq + n_seq - k) % n_seq
        here = dst_buf.at[block(origin, CAP), :]
        pltpu.make_async_remote_copy(
            src_ref=here, dst_ref=here, send_sem=sends.at[k], recv_sem=recvs.at[k],
            device_id=(dp, origin), device_id_type=MESH,
        ).wait_recv()

    local[0].wait()
    sendb[:, :width] = dot(place[...], hid[...]).astype(BF)
    for k in (2, 1, 3):
        copy = exchange(sendb, recvb, s_send, s_recv, k)
        copy.start()
        pending.append(copy)
    recvb[block(seq, CAP), :] = sendb[block(seq, CAP), :]

    for a in (0, 1, 2):
        forward_first(a)
    own(3)
    for a in (0, 1, 2):
        forward_second(a)

    for k in (1, 2, 3):
        arrival(sendb, recvb, s_send, s_recv, k)
    lanes = lax.broadcasted_iota(jnp.int32, (n_seq * CAP, 128), 1).astype(F32)
    unplace[...] = (recvb[:, width:].astype(F32) == lanes).astype(F32).astype(BF)
    x_float = dot(unplace[...], recvb[:, :width], 0, 0)
    packed[...] = x_float
    inv_pre = lax.rsqrt(jnp.mean(x_float * x_float, axis=-1, keepdims=True) + epsilon)
    normed[...] = (x_float * inv_pre * gain_b_ref[...]).astype(BF)

    for a in (0, 1, 2):
        forward_diag(a)
    for copy in local[1:]:
        copy.wait()
    for a in (0, 1, 2):
        finish(a)

    low[...] = dot(normed[...], dn[...]).astype(BF)

    tile = 256

    @pl.loop(0, proj.shape[1] // tile)
    def _(n):
        at = pl.ds(pl.multiple_of(n * tile, tile), tile)
        proj[:, at] = (
            dot(normed[...], wv[:, at]) + dot(low[...], up[at, :], 1, 1)
        ).astype(BF)

    forward_first(3)
    forward_second(3)
    forward_diag(3)
    finish(3)

    @pl.loop(0, width // tile)
    def _(n):
        at = pl.ds(pl.multiple_of(n * tile, tile), tile)
        mixed[:, at] = dot(proj[...], wo[:, at])

    m = mixed[...]
    inv_post = lax.rsqrt(jnp.mean(m * m, axis=-1, keepdims=True) + epsilon)
    shaped = m * inv_post
    gain_a = gain_a_ref[...]
    looped[...] = (packed[...] + shaped * gain_a).astype(BF)
    loop_out = pltpu.make_async_copy(looped, looped_hbm, loc.at[6])
    loop_out.start()
    grad_shaped = cot[...].astype(F32) * gain_a
    mixed[...] = inv_post * (
        grad_shaped - shaped * jnp.mean(grad_shaped * shaped, axis=-1, keepdims=True)
    )

    @pl.loop(0, gv.shape[1] // tile)
    def _(n):
        at = pl.ds(pl.multiple_of(n * tile, tile), tile)
        gv[:, at] = dot(mixed[...].astype(BF), wo[at, :], 1, 1).astype(BF)

    grad_low = dot(gv[...], up[...]).astype(BF)

    down_rows, up_rows = down_out.shape[0], up_out.shape[0]
    down_term = dot(normed[...], grad_low, 0, 0).astype(BF)
    up_term = dot(gv[...], low[...], 0, 0).astype(BF)
    for owner in range(n_dp):
        lsend[owner, :down_rows, :] = down_term[owner * down_rows : (owner + 1) * down_rows, :]
        lsend[owner, down_rows:, :] = up_term[owner * up_rows : (owner + 1) * up_rows, :]
    for k in range(1, n_dp):
        target = (dp + k) % n_dp
        copy = pltpu.make_async_remote_copy(
            src_ref=lsend.at[target], dst_ref=lrecv.at[dp], send_sem=l_send.at[k],
            recv_sem=l_recv.at[k], device_id=(target, seq), device_id_type=MESH,
        )
        copy.start()
        pending.append(copy)
    lrecv[dp] = lsend[dp]

    @pl.loop(0, width // tile)
    def _(n):
        at = pl.ds(pl.multiple_of(n * tile, tile), tile)
        gn[:, at] = dot(gv[...], wv[at, :], 1, 1) + dot(grad_low, dn[at, :], 1, 1)

    x_float = packed[...]
    inv_pre = lax.rsqrt(jnp.mean(x_float * x_float, axis=-1, keepdims=True) + epsilon)
    whitened = x_float * inv_pre
    grad_white = gn[...] * gain_b_ref[...]
    grad_packed = (
        cot[...].astype(F32)
        + inv_pre
        * (grad_white - whitened * jnp.mean(grad_white * whitened, axis=-1, keepdims=True))
    ).astype(BF)
    gsend[...] = dot(unplace[...], grad_packed).astype(BF)
    for k in (2, 1, 3):
        copy = exchange(gsend, grecv, g_send, g_recv, k)
        copy.start()
        pending.append(copy)
    grecv[block(seq, CAP), :] = gsend[block(seq, CAP), :]

    for k in range(1, n_dp):
        origin = (dp + n_dp - k) % n_dp
        here = lrecv.at[origin]
        pltpu.make_async_remote_copy(
            src_ref=here, dst_ref=here, send_sem=l_send.at[k], recv_sem=l_recv.at[k],
            device_id=(origin, seq), device_id_type=MESH,
        ).wait_recv()
    total = lrecv[0].astype(F32)
    for owner in range(1, n_dp):
        total += lrecv[owner].astype(F32)
    lead = total.shape[0]
    pad = zsend.shape[1] - lead
    total = jnp.concatenate([total, jnp.zeros((pad, total.shape[1]), F32)], axis=0)
    zsend[...] = total.T
    cols = down_out.shape[1]
    for k in range(1, n_seq):
        target = (seq + k) % n_seq
        copy = pltpu.make_async_remote_copy(
            src_ref=zsend.at[pl.ds(pl.multiple_of(target * cols, 8), cols), :],
            dst_ref=zrecv.at[seq], send_sem=z_send.at[k], recv_sem=z_recv.at[k],
            device_id=(dp, target), device_id_type=MESH,
        )
        copy.start()
        pending.append(copy)
    zrecv[seq] = zsend[pl.ds(pl.multiple_of(seq * cols, 8), cols), :]

    for k in (1, 2, 3):
        arrival(gsend, grecv, g_send, g_recv, k)
    hid[...] = dot(place[...], grecv[...], 0, 0).astype(BF)
    grad_out = pltpu.make_async_copy(hid, gh_hbm, loc.at[7])
    grad_out.start()

    for k in range(1, n_seq):
        origin = (seq + n_seq - k) % n_seq
        here = zrecv.at[origin]
        pltpu.make_async_remote_copy(
            src_ref=here, dst_ref=here, send_sem=z_send.at[k], recv_sem=z_recv.at[k],
            device_id=(dp, origin), device_id_type=MESH,
        ).wait_recv()
    grad_scale = 1.0 / math.sqrt(n_seq * cot.shape[0] * n_dp)
    mine = ((zrecv[0] + zrecv[1]) + (zrecv[2] + zrecv[3])) * grad_scale
    mine = jnp.concatenate([mine, jnp.zeros((128 - cols, mine.shape[1]), F32)], axis=0).T
    down_out[...] = mine[:down_rows, :cols]
    up_out[...] = mine[down_rows:lead, :cols]
    for copy in pending:
        copy.wait_send()
    loop_out.wait()
    grad_out.wait()


def fused_body(
    hidden, depths, packed_slot_index, value_weight, output_weight, adapter_down_factor,
    adapter_up_factor, before_norm_gain, after_norm_gain, cotangent,
):
    tok, width = hidden.shape
    act = cotangent.shape[0]
    n_dp, n_seq = lax.axis_size("dp"), lax.axis_size("seq")
    v_rows, value_width = value_weight.shape
    o_rows = output_weight.shape[0]
    rank = adapter_up_factor.shape[1]
    u_rows = adapter_up_factor.shape[0]
    cols = rank // n_seq
    lead = v_rows + u_rows
    lead_pad = -(-lead // 128) * 128
    vm, hbm = pl.BlockSpec(memory_space=pltpu.VMEM), pl.BlockSpec(memory_space=pl.ANY)
    dma = pltpu.SemaphoreType.DMA
    rows = n_seq * CAP
    return pl.pallas_call(
        fused_kernel,
        out_shape=(
            jax.ShapeDtypeStruct((act, width), BF),
            jax.ShapeDtypeStruct((tok, width), BF),
            jax.ShapeDtypeStruct((v_rows, cols), F32),
            jax.ShapeDtypeStruct((u_rows, cols), F32),
        ),
        in_specs=[vm] * 4 + [hbm] * 6,
        out_specs=(hbm, hbm, vm, vm),
        scratch_shapes=[
            pltpu.VMEM((v_rows * n_dp, value_width), BF),
            pltpu.VMEM((o_rows * n_dp, width), BF),
            pltpu.VMEM((v_rows * n_dp, rank), BF),
            pltpu.VMEM((u_rows * n_dp, rank), BF),
            pltpu.VMEM((tok, width), BF),
            pltpu.VMEM((act, width), BF),
            pltpu.VMEM((rows, width + 128), BF),
            pltpu.VMEM((rows, width + 128), BF),
            pltpu.VMEM((rows, width), BF),
            pltpu.VMEM((rows, width), BF),
            pltpu.VMEM((n_dp, lead, rank), BF),
            pltpu.VMEM((n_dp, lead, rank), BF),
            pltpu.VMEM((rank, lead_pad), F32),
            pltpu.VMEM((n_seq, cols, lead_pad), F32),
            pltpu.VMEM((rows, tok), BF),
            pltpu.VMEM((rows, 128), BF),
            pltpu.VMEM((act, width), BF),
            pltpu.VMEM((act, rank), BF),
            pltpu.VMEM((act, value_width), BF),
            pltpu.VMEM((act, width), F32),
            pltpu.VMEM((act, value_width), BF),
            pltpu.VMEM((act, width), F32),
            pltpu.VMEM((act, width), F32),
            pltpu.VMEM((act, width), BF),
            dma((52,)), dma((52,)), dma((4,)), dma((4,)), dma((8,)), dma((8,)),
            dma((4,)), dma((4,)), dma((4,)), dma((4,)), dma((8,)),
        ],
        compiler_params=pltpu.CompilerParams(
            collective_id=0, has_side_effects=True, vmem_limit_bytes=48 << 20
        ),
    )(
        packed_slot_index.reshape(1, tok),
        depths.reshape(1, tok),
        before_norm_gain.reshape(1, width),
        after_norm_gain.reshape(1, width),
        hidden,
        cotangent,
        value_weight,
        output_weight,
        adapter_down_factor,
        adapter_up_factor,
    )


def body(*arrays):
    fits = (
        lax.axis_size("dp") == 8
        and lax.axis_size("seq") == 4
        and arrays[0].shape[0] == 4 * CAP
        and arrays[9].shape[0] == 128
        and arrays[0].shape[1] % 256 == 0
        and arrays[3].shape[1] % 256 == 0
        and all(arrays[i].shape[0] % 32 == 0 for i in (3, 4, 5, 6))
        and arrays[6].shape[1] == 128
    )
    return (fused_body if fits else general_body)(*arrays)


def solution(mesh):
    placed = (
        P(("dp", "seq"), None),
        P(("dp", "seq")),
        P(("dp", "seq")),
        P("dp", None),
        P("dp", None),
        P("dp", None),
        P("dp", None),
        P(),
        P(),
        P(("dp", "seq"), None),
    )
    return jax.shard_map(
        body,
        mesh=mesh,
        in_specs=placed,
        out_specs=(P(("dp", "seq"), None), P(("dp", "seq"), None), P("dp", "seq"), P("dp", "seq")),
        check_vma=False,
    )
```

```python
import functools
import math

import jax
import jax.numpy as jnp
from jax import lax
from jax.experimental import pallas as pl
from jax.experimental.pallas import tpu as pltpu
from jax.sharding import PartitionSpec as P

epsilon = 1e-06


def contract_final_axis(left, right):
    return lax.dot_general(
        left, right, (((1,), (1,)), ((), ())), preferred_element_type=jnp.float32
    )


def contract_first(left, right):
    return lax.dot_general(
        left, right, (((0,), (0,)), ((), ())), preferred_element_type=jnp.float32
    )


def layer_forward(
    input_rows,
    cotangent_rows,
    value_weight,
    output_weight,
    adapter_down_factor,
    adapter_up_factor,
    before_norm_gain,
    after_norm_gain,
):
    x_float = input_rows.astype(jnp.float32)
    inv_pre = lax.rsqrt(jnp.mean(x_float * x_float, axis=-1, keepdims=True) + epsilon)
    whitened = x_float * inv_pre
    normalized_rows = (whitened * before_norm_gain).astype(jnp.bfloat16)
    rank_reduced = jnp.dot(
        normalized_rows, adapter_down_factor, preferred_element_type=jnp.float32
    ).astype(jnp.bfloat16)
    projected_rows = (
        jnp.dot(normalized_rows, value_weight, preferred_element_type=jnp.float32)
        + contract_final_axis(rank_reduced, adapter_up_factor)
    ).astype(jnp.bfloat16)
    mixed_out = jnp.dot(projected_rows, output_weight, preferred_element_type=jnp.float32)
    inv_post = lax.rsqrt(jnp.mean(mixed_out * mixed_out, axis=-1, keepdims=True) + epsilon)
    shaped = mixed_out * inv_post
    looped = (x_float + shaped * after_norm_gain).astype(jnp.bfloat16)
    cot_float = cotangent_rows.astype(jnp.float32)
    grad_shaped = cot_float * after_norm_gain
    grad_mixed = (
        inv_post * (grad_shaped - shaped * jnp.mean(grad_shaped * shaped, axis=-1, keepdims=True))
    ).astype(jnp.bfloat16)
    value_gradient = contract_final_axis(grad_mixed, output_weight).astype(jnp.bfloat16)
    low_rank_gradient = jnp.dot(
        value_gradient, adapter_up_factor, preferred_element_type=jnp.float32
    ).astype(jnp.bfloat16)
    normalized_gradient = contract_final_axis(value_gradient, value_weight) + contract_final_axis(
        low_rank_gradient, adapter_down_factor
    )
    grad_white = normalized_gradient * before_norm_gain
    gradient_rows = (
        cot_float
        + inv_pre
        * (grad_white - whitened * jnp.mean(grad_white * whitened, axis=-1, keepdims=True))
    ).astype(jnp.bfloat16)
    down_factor_gradient = contract_first(normalized_rows, low_rank_gradient)
    up_factor_gradient = contract_first(value_gradient, rank_reduced)
    return (looped, gradient_rows, down_factor_gradient, up_factor_gradient)


def general_body(
    hidden,
    depths,
    packed_slot_index,
    value_weight,
    output_weight,
    adapter_down_factor,
    adapter_up_factor,
    before_norm_gain,
    after_norm_gain,
    cotangent,
):
    seq_count = lax.axis_size("seq")
    own_index = lax.axis_index("seq")
    tok_count = hidden.shape[0]
    act_rows = cotangent.shape[0]
    value_full, out_full, down_full, up_full = (
        lax.all_gather(value_weight, "dp", axis=0, tiled=True),
        lax.all_gather(output_weight, "dp", axis=0, tiled=True),
        lax.all_gather(adapter_down_factor, "dp", axis=0, tiled=True),
        lax.all_gather(adapter_up_factor, "dp", axis=0, tiled=True),
    )
    depth_all, slot_all = (
        lax.all_gather(depths, "seq", axis=0, tiled=True),
        lax.all_gather(packed_slot_index, "seq", axis=0, tiled=True),
    )
    active_all = depth_all >= 2
    dest_all = jnp.where(active_all, slot_all // act_rows, -1)
    pos_all = jnp.where(active_all, slot_all % act_rows, 0)
    mine = active_all & (dest_all == own_index)
    active = depths >= 2
    zero_row = jnp.zeros((), jnp.bfloat16)
    rows_all = lax.all_gather(hidden, "seq", axis=0, tiled=True)
    source = (
        jnp.zeros((act_rows,), jnp.int32)
        .at[jnp.where(mine, pos_all, act_rows)]
        .set(jnp.arange(seq_count * tok_count, dtype=jnp.int32), mode="drop")
    )
    packed = jnp.take(rows_all, source, axis=0)
    looped, gradient_rows, down_factor_gradient, up_factor_gradient = layer_forward(
        packed,
        cotangent,
        value_full,
        out_full,
        down_full,
        up_full,
        before_norm_gain,
        after_norm_gain,
    )
    grads_all = lax.all_gather(gradient_rows, "seq", axis=0, tiled=True)
    picked = jnp.take(grads_all, jnp.maximum(packed_slot_index, 0), axis=0)
    grad_hidden = jnp.where(active[:, None], picked, zero_row)
    grad_scale = 1.0 / math.sqrt(seq_count * act_rows * lax.axis_size("dp"))
    down_term = down_factor_gradient * grad_scale
    up_term = up_factor_gradient * grad_scale
    down_mid, up_mid = (
        lax.psum_scatter(
            down_term.astype(jnp.bfloat16), "seq", scatter_dimension=1, tiled=True
        ).astype(jnp.float32),
        lax.psum_scatter(
            up_term.astype(jnp.bfloat16), "seq", scatter_dimension=1, tiled=True
        ).astype(jnp.float32),
    )
    down_sum, up_sum = (
        lax.psum_scatter(down_mid, "dp", scatter_dimension=0, tiled=True),
        lax.psum_scatter(up_mid, "dp", scatter_dimension=0, tiled=True),
    )
    return (looped, grad_hidden, down_sum, up_sum)


MESH = pl.DeviceIdType.MESH
BF, F32 = jnp.bfloat16, jnp.float32
CAP = 64


def dot(left, right, left_axis=1, right_axis=0):
    return lax.dot_general(
        left, right, (((left_axis,), (right_axis,)), ((), ())), preferred_element_type=F32
    )


def fused_kernel(
    slot_ref, depth_ref, gain_b_ref, gain_a_ref, hidden_hbm, cot_hbm, wv_in, wo_in, dn_in, up_in,
    looped_hbm, gh_hbm, lora_out,
    wv, wo, dn, up, hid, cot, sendb, recvb, gsend, grecv, lsend, lrecv, zsend, zrecv,
    place, unplace, normed, low, proj, mixed, gv, gn, packed, looped,
    w_send, w_recv, s_send, s_recv, l_send, l_recv, g_send, g_recv, z_send, z_recv, loc,
):
    dp, seq = lax.axis_index("dp"), lax.axis_index("seq")
    n_dp, n_seq = 8, 4
    width = hid.shape[1]
    core, x, y = dp % 2, (dp // 2) % 2, dp // 4
    nbr_x, nbr_y, sib = dp + 2 - 4 * x, dp + 4 - 8 * y, dp + 1 - 2 * core
    diag = nbr_x + 4 - 8 * y
    to_sib = 1 - 2 * core
    partner = seq + 1 - 2 * (seq % 2)
    side = (core + seq) % 2
    turn_from = nbr_x + side * (nbr_y - nbr_x)
    turn_to = nbr_y + side * (nbr_x - nbr_y)

    local = [
        pltpu.make_async_copy(hidden_hbm, hid, loc.at[0]),
        pltpu.make_async_copy(cot_hbm, cot, loc.at[1]),
    ]
    arrays = [(dn_in, dn), (up_in, up), (wv_in, wv), (wo_in, wo)]
    for number, (shard, full) in enumerate(arrays):
        rows = shard.shape[0]
        local.append(
            pltpu.make_async_copy(
                shard, full.at[pl.ds(pl.multiple_of(dp * rows, 16), rows), :], loc.at[2 + number]
            )
        )
    for copy in local:
        copy.start()

    barrier = pltpu.get_barrier_semaphore()
    for k in range(1, n_dp):
        pl.semaphore_signal(barrier, inc=1, device_id=((dp + k) % n_dp, seq), device_id_type=MESH)
    for k in range(1, n_seq):
        pl.semaphore_signal(barrier, inc=1, device_id=(dp, (seq + k) % n_seq), device_id_type=MESH)

    tok = hid.shape[0]
    slots = slot_ref[...]
    act = depth_ref[...] >= 2
    dest = jnp.where(act, slots // 128, -1)
    where_to = lax.broadcasted_iota(jnp.int32, (8, tok), 0) == dest
    earlier = (
        lax.broadcasted_iota(jnp.int32, (tok, tok), 0)
        < lax.broadcasted_iota(jnp.int32, (tok, tok), 1)
    ).astype(F32).astype(BF)
    counts = dot(where_to.astype(F32).astype(BF), earlier)
    rank = jnp.sum(jnp.where(where_to, counts, 0.0), axis=0, keepdims=True)
    row_of = jnp.where(act, dest.astype(F32) * CAP + rank, -1.0)
    picked = (lax.broadcasted_iota(jnp.int32, (n_seq * CAP, tok), 0).astype(F32) == row_of).astype(F32)
    place[...] = picked.astype(BF)
    position = jnp.where(act, slots - dest * 128 + 1, 0).astype(F32)
    pos_col = jnp.sum(picked * position, axis=1, keepdims=True) - 1.0
    sendb[:, width:] = jnp.broadcast_to(pos_col, (n_seq * CAP, 128)).astype(BF)

    pl.semaphore_wait(barrier, n_dp - 1 + n_seq - 1)

    def region(a, owner, half):
        shard, full = arrays[a]
        rows = shard.shape[0]
        if half is None:
            return full.at[pl.ds(pl.multiple_of(owner * rows, 16), rows), :]
        part = rows // 2
        return full.at[pl.ds(pl.multiple_of(owner * rows + half * part, 16), part), :]

    def piece(a, number, owner, half, target, from_input=False, at_seq=None):
        dst = region(a, owner, half)
        if from_input:
            shard = arrays[a][0]
            part = shard.shape[0] // 2
            source = shard if half is None else shard.at[pl.ds(half * part, part), :]
        else:
            source = dst
        return pltpu.make_async_remote_copy(
            src_ref=source, dst_ref=dst, send_sem=w_send.at[a * 13 + number],
            recv_sem=w_recv.at[a * 13 + number],
            device_id=(target, seq if at_seq is None else at_seq), device_id_type=MESH,
        )

    pending = []

    def send(*args, **kw):
        copy = piece(*args, **kw)
        copy.start()
        pending.append(copy)

    def got(a, number, owner, half):
        piece(a, number, owner, half, sib).wait_recv()

    def own_first(a):
        send(a, 0, dp, 0, nbr_x, from_input=True)
        send(a, 3, dp, 1, nbr_y, from_input=True)
        send(a, 6, dp, None, sib, from_input=True)

    def own_second(a):
        send(a, 1, dp, 1, nbr_x, from_input=True)
        send(a, 2, dp, 0, nbr_y, from_input=True)

    def forward_first(a):
        got(a, 0, nbr_x, 0)
        got(a, 3, nbr_y, 1)
        send(a, 4, turn_from, side, turn_to)
        send(a, 7, nbr_x, 0, sib)
        send(a, 8, nbr_y, 1, sib)

    def forward_second(a):
        got(a, 1, nbr_x, 1)
        send(a, 9, nbr_x, 1, sib)
        got(a, 2, nbr_y, 0)
        send(a, 10, nbr_y, 0, sib)

    def forward_diag(a):
        got(a, 4, diag, side)
        send(a, 5, diag, side, dp, at_seq=partner)
        send(a, 11, diag, side, sib)

    def forward_partner(a):
        got(a, 5, diag, 1 - side)
        send(a, 12, diag, 1 - side, sib)

    def finish(a):
        got(a, 6, sib, None)
        got(a, 7, nbr_x + to_sib, 0)
        got(a, 8, nbr_y + to_sib, 1)
        got(a, 9, nbr_x + to_sib, 1)
        got(a, 10, nbr_y + to_sib, 0)
        got(a, 11, diag + to_sib, 1 - side)
        got(a, 12, diag + to_sib, side)

    for a in (0, 1, 2, 3):
        own_first(a)

    def block(owner, rows):
        return pl.ds(pl.multiple_of(owner * rows, 16), rows)

    def exchange(src_buf, dst_buf, sends, recvs, k):
        target = (seq + k) % n_seq
        return pltpu.make_async_remote_copy(
            src_ref=src_buf.at[block(target, CAP), :], dst_ref=dst_buf.at[block(seq, CAP), :],
            send_sem=sends.at[k], recv_sem=recvs.at[k], device_id=(dp, target), device_id_type=MESH,
        )

    def arrival(src_buf, dst_buf, sends, recvs, k):
        origin = (seq + n_seq - k) % n_seq
        here = dst_buf.at[block(origin, CAP), :]
        pltpu.make_async_remote_copy(
            src_ref=here, dst_ref=here, send_sem=sends.at[k], recv_sem=recvs.at[k],
            device_id=(dp, origin), device_id_type=MESH,
        ).wait_recv()

    local[0].wait()
    sendb[:, :width] = dot(place[...], hid[...]).astype(BF)
    for k in (2, 1, 3):
        copy = exchange(sendb, recvb, s_send, s_recv, k)
        copy.start()
        pending.append(copy)
    recvb[block(seq, CAP), :] = sendb[block(seq, CAP), :]

    for a in (0, 1, 2):
        forward_first(a)
    for a in (0, 1, 2):
        own_second(a)
    forward_first(3)
    own_second(3)
    for a in (0, 1, 2):
        forward_diag(a)
    for a in (0, 1, 2):
        forward_second(a)
    forward_diag(3)
    for a in (0, 1, 2):
        forward_partner(a)

    for k in (1, 2, 3):
        arrival(sendb, recvb, s_send, s_recv, k)
    lanes = lax.broadcasted_iota(jnp.int32, (n_seq * CAP, 128), 1).astype(F32)
    unplace[...] = (recvb[:, width:].astype(F32) == lanes).astype(F32).astype(BF)
    x_float = dot(unplace[...], recvb[:, :width], 0, 0)
    packed[...] = x_float
    inv_pre = lax.rsqrt(jnp.mean(x_float * x_float, axis=-1, keepdims=True) + epsilon)
    normed[...] = (x_float * inv_pre * gain_b_ref[...].reshape(1, width)).astype(BF)

    for copy in local[1:]:
        copy.wait()
    for a in (0, 1, 2):
        finish(a)

    low[...] = dot(normed[...], dn[...]).astype(BF)

    tile = 256

    @pl.loop(0, proj.shape[1] // tile)
    def _(n):
        at = pl.ds(pl.multiple_of(n * tile, tile), tile)
        proj[:, at] = (
            dot(normed[...], wv[:, at]) + dot(low[...], up[at, :], 1, 1)
        ).astype(BF)

    forward_second(3)
    forward_partner(3)
    finish(3)

    @pl.loop(0, width // tile)
    def _(n):
        at = pl.ds(pl.multiple_of(n * tile, tile), tile)
        mixed[:, at] = dot(proj[...], wo[:, at])

    m = mixed[...]
    inv_post = lax.rsqrt(jnp.mean(m * m, axis=-1, keepdims=True) + epsilon)
    shaped = m * inv_post
    gain_a = gain_a_ref[...].reshape(1, width)
    looped[...] = (packed[...] + shaped * gain_a).astype(BF)
    loop_out = pltpu.make_async_copy(looped, looped_hbm, loc.at[6])
    loop_out.start()
    grad_shaped = cot[...].astype(F32) * gain_a
    mixed[...] = inv_post * (
        grad_shaped - shaped * jnp.mean(grad_shaped * shaped, axis=-1, keepdims=True)
    )

    @pl.loop(0, gv.shape[1] // tile)
    def _(n):
        at = pl.ds(pl.multiple_of(n * tile, tile), tile)
        gv[:, at] = dot(mixed[...].astype(BF), wo[at, :], 1, 1).astype(BF)

    grad_low = dot(gv[...], up[...]).astype(BF)

    @pl.loop(0, width // tile)
    def _(n):
        at = pl.ds(pl.multiple_of(n * tile, tile), tile)
        gn[:, at] = dot(gv[...], wv[at, :], 1, 1) + dot(grad_low, dn[at, :], 1, 1)

    x_float = packed[...]
    inv_pre = lax.rsqrt(jnp.mean(x_float * x_float, axis=-1, keepdims=True) + epsilon)
    whitened = x_float * inv_pre
    grad_white = gn[...] * gain_b_ref[...].reshape(1, width)
    grad_packed = (
        cot[...].astype(F32)
        + inv_pre
        * (grad_white - whitened * jnp.mean(grad_white * whitened, axis=-1, keepdims=True))
    ).astype(BF)
    gsend[...] = dot(unplace[...], grad_packed).astype(BF)
    for k in (2, 1, 3):
        copy = exchange(gsend, grecv, g_send, g_recv, k)
        copy.start()
        pending.append(copy)
    grecv[block(seq, CAP), :] = gsend[block(seq, CAP), :]

    down_rows, up_rows = dn_in.shape[0], up_in.shape[0]
    down_term = dot(normed[...], grad_low, 0, 0).astype(BF)
    up_term = dot(gv[...], low[...], 0, 0).astype(BF)
    for owner in range(n_dp):
        lsend[owner, :down_rows, :] = down_term[owner * down_rows : (owner + 1) * down_rows, :]
        lsend[owner, down_rows:, :] = up_term[owner * up_rows : (owner + 1) * up_rows, :]
    for k in range(1, n_dp):
        target = (dp + k) % n_dp
        copy = pltpu.make_async_remote_copy(
            src_ref=lsend.at[target], dst_ref=lrecv.at[dp], send_sem=l_send.at[k],
            recv_sem=l_recv.at[k], device_id=(target, seq), device_id_type=MESH,
        )
        copy.start()
        pending.append(copy)
    lrecv[dp] = lsend[dp]

    for k in range(1, n_dp):
        origin = (dp + n_dp - k) % n_dp
        here = lrecv.at[origin]
        pltpu.make_async_remote_copy(
            src_ref=here, dst_ref=here, send_sem=l_send.at[k], recv_sem=l_recv.at[k],
            device_id=(origin, seq), device_id_type=MESH,
        ).wait_recv()
    total = lrecv[0].astype(F32)
    for owner in range(1, n_dp):
        total += lrecv[owner].astype(F32)
    lead = total.shape[0]
    pad = zsend.shape[1] - lead
    total = jnp.concatenate([total, jnp.zeros((pad, total.shape[1]), F32)], axis=0)
    zsend[...] = total.T.astype(BF)
    cols = lora_out.shape[0]
    for k in range(1, n_seq):
        target = (seq + k) % n_seq
        copy = pltpu.make_async_remote_copy(
            src_ref=zsend.at[pl.ds(pl.multiple_of(target * cols, 16), cols), :],
            dst_ref=zrecv.at[seq], send_sem=z_send.at[k], recv_sem=z_recv.at[k],
            device_id=(dp, target), device_id_type=MESH,
        )
        copy.start()
        pending.append(copy)
    zrecv[seq] = zsend[pl.ds(pl.multiple_of(seq * cols, 16), cols), :]

    for k in (1, 2, 3):
        arrival(gsend, grecv, g_send, g_recv, k)
    hid[...] = dot(place[...], grecv[...], 0, 0).astype(BF)
    grad_out = pltpu.make_async_copy(hid, gh_hbm, loc.at[7])
    grad_out.start()

    for k in range(1, n_seq):
        origin = (seq + n_seq - k) % n_seq
        here = zrecv.at[origin]
        pltpu.make_async_remote_copy(
            src_ref=here, dst_ref=here, send_sem=z_send.at[k], recv_sem=z_recv.at[k],
            device_id=(dp, origin), device_id_type=MESH,
        ).wait_recv()
    grad_scale = 1.0 / math.sqrt(n_seq * cot.shape[0] * n_dp)
    z = [zrecv[owner].astype(F32) for owner in range(n_seq)]
    lora_out[...] = ((z[0] + z[1]) + (z[2] + z[3])) * grad_scale
    for copy in pending:
        copy.wait_send()
    loop_out.wait()
    grad_out.wait()


def fused_body(
    hidden, depths, packed_slot_index, value_weight, output_weight, adapter_down_factor,
    adapter_up_factor, before_norm_gain, after_norm_gain, cotangent,
):
    tok, width = hidden.shape
    act = cotangent.shape[0]
    n_dp, n_seq = lax.axis_size("dp"), lax.axis_size("seq")
    v_rows, value_width = value_weight.shape
    o_rows = output_weight.shape[0]
    rank = adapter_up_factor.shape[1]
    u_rows = adapter_up_factor.shape[0]
    cols = rank // n_seq
    lead = v_rows + u_rows
    lead_pad = -(-lead // 128) * 128
    vm, hbm = pl.BlockSpec(memory_space=pltpu.VMEM), pl.BlockSpec(memory_space=pltpu.HBM)
    dma = pltpu.SemaphoreType.DMA
    rows = n_seq * CAP
    looped, grad_hidden, lora = pl.pallas_call(
        fused_kernel,
        out_shape=(
            jax.ShapeDtypeStruct((act, width), BF),
            jax.ShapeDtypeStruct((tok, width), BF),
            jax.ShapeDtypeStruct((cols, lead_pad), F32),
        ),
        in_specs=[vm] * 4 + [hbm] * 6,
        out_specs=(hbm, hbm, vm),
        scratch_shapes=[
            pltpu.VMEM((v_rows * n_dp, value_width), BF),
            pltpu.VMEM((o_rows * n_dp, width), BF),
            pltpu.VMEM((v_rows * n_dp, rank), BF),
            pltpu.VMEM((u_rows * n_dp, rank), BF),
            pltpu.VMEM((tok, width), BF),
            pltpu.VMEM((act, width), BF),
            pltpu.VMEM((rows, width + 128), BF),
            pltpu.VMEM((rows, width + 128), BF),
            pltpu.VMEM((rows, width), BF),
            pltpu.VMEM((rows, width), BF),
            pltpu.VMEM((n_dp, lead, rank), BF),
            pltpu.VMEM((n_dp, lead, rank), BF),
            pltpu.VMEM((rank, lead_pad), BF),
            pltpu.VMEM((n_seq, cols, lead_pad), BF),
            pltpu.VMEM((rows, tok), BF),
            pltpu.VMEM((rows, 128), BF),
            pltpu.VMEM((act, width), BF),
            pltpu.VMEM((act, rank), BF),
            pltpu.VMEM((act, value_width), BF),
            pltpu.VMEM((act, width), F32),
            pltpu.VMEM((act, value_width), BF),
            pltpu.VMEM((act, width), F32),
            pltpu.VMEM((act, width), F32),
            pltpu.VMEM((act, width), BF),
            dma((52,)), dma((52,)), dma((4,)), dma((4,)), dma((8,)), dma((8,)),
            dma((4,)), dma((4,)), dma((4,)), dma((4,)), dma((8,)),
        ],
        compiler_params=pltpu.CompilerParams(
            collective_id=0, has_side_effects=True, vmem_limit_bytes=62 << 20
        ),
    )(
        packed_slot_index.reshape(1, tok),
        depths.reshape(1, tok),
        before_norm_gain,
        after_norm_gain,
        hidden,
        cotangent,
        value_weight,
        output_weight,
        adapter_down_factor,
        adapter_up_factor,
    )
    return looped, grad_hidden, lora[:, :v_rows].T, lora[:, v_rows:lead].T


def body(*arrays):
    fits = (
        lax.axis_size("dp") == 8
        and lax.axis_size("seq") == 4
        and arrays[0].shape[0] == 4 * CAP
        and arrays[9].shape[0] == 128
        and arrays[0].shape[1] % 256 == 0
        and arrays[3].shape[1] % 256 == 0
        and all(arrays[i].shape[0] % 32 == 0 for i in (3, 4, 5, 6))
        and arrays[6].shape[1] == 128
    )
    return (fused_body if fits else general_body)(*arrays)


def solution(mesh):
    placed = (
        P(("dp", "seq"), None),
        P(("dp", "seq")),
        P(("dp", "seq")),
        P("dp", None),
        P("dp", None),
        P("dp", None),
        P("dp", None),
        P(),
        P(),
        P(("dp", "seq"), None),
    )
    return jax.shard_map(
        body,
        mesh=mesh,
        in_specs=placed,
        out_specs=(P(("dp", "seq"), None), P(("dp", "seq"), None), P("dp", "seq"), P("dp", "seq")),
        check_vma=False,
    )
```

```python
import functools
import math

import jax
import jax.numpy as jnp
from jax import lax
from jax.experimental import pallas as pl
from jax.experimental.pallas import tpu as pltpu
from jax.sharding import PartitionSpec as P

epsilon = 1e-06


def contract_final_axis(left, right):
    return lax.dot_general(
        left, right, (((1,), (1,)), ((), ())), preferred_element_type=jnp.float32
    )


def contract_first(left, right):
    return lax.dot_general(
        left, right, (((0,), (0,)), ((), ())), preferred_element_type=jnp.float32
    )


def layer_forward(
    input_rows,
    cotangent_rows,
    value_weight,
    output_weight,
    adapter_down_factor,
    adapter_up_factor,
    before_norm_gain,
    after_norm_gain,
):
    x_float = input_rows.astype(jnp.float32)
    inv_pre = lax.rsqrt(jnp.mean(x_float * x_float, axis=-1, keepdims=True) + epsilon)
    whitened = x_float * inv_pre
    normalized_rows = (whitened * before_norm_gain).astype(jnp.bfloat16)
    rank_reduced = jnp.dot(
        normalized_rows, adapter_down_factor, preferred_element_type=jnp.float32
    ).astype(jnp.bfloat16)
    projected_rows = (
        jnp.dot(normalized_rows, value_weight, preferred_element_type=jnp.float32)
        + contract_final_axis(rank_reduced, adapter_up_factor)
    ).astype(jnp.bfloat16)
    mixed_out = jnp.dot(projected_rows, output_weight, preferred_element_type=jnp.float32)
    inv_post = lax.rsqrt(jnp.mean(mixed_out * mixed_out, axis=-1, keepdims=True) + epsilon)
    shaped = mixed_out * inv_post
    looped = (x_float + shaped * after_norm_gain).astype(jnp.bfloat16)
    cot_float = cotangent_rows.astype(jnp.float32)
    grad_shaped = cot_float * after_norm_gain
    grad_mixed = (
        inv_post * (grad_shaped - shaped * jnp.mean(grad_shaped * shaped, axis=-1, keepdims=True))
    ).astype(jnp.bfloat16)
    value_gradient = contract_final_axis(grad_mixed, output_weight).astype(jnp.bfloat16)
    low_rank_gradient = jnp.dot(
        value_gradient, adapter_up_factor, preferred_element_type=jnp.float32
    ).astype(jnp.bfloat16)
    normalized_gradient = contract_final_axis(value_gradient, value_weight) + contract_final_axis(
        low_rank_gradient, adapter_down_factor
    )
    grad_white = normalized_gradient * before_norm_gain
    gradient_rows = (
        cot_float
        + inv_pre
        * (grad_white - whitened * jnp.mean(grad_white * whitened, axis=-1, keepdims=True))
    ).astype(jnp.bfloat16)
    down_factor_gradient = contract_first(normalized_rows, low_rank_gradient)
    up_factor_gradient = contract_first(value_gradient, rank_reduced)
    return (looped, gradient_rows, down_factor_gradient, up_factor_gradient)


def general_body(
    hidden,
    depths,
    packed_slot_index,
    value_weight,
    output_weight,
    adapter_down_factor,
    adapter_up_factor,
    before_norm_gain,
    after_norm_gain,
    cotangent,
):
    seq_count = lax.axis_size("seq")
    own_index = lax.axis_index("seq")
    tok_count = hidden.shape[0]
    act_rows = cotangent.shape[0]
    value_full, out_full, down_full, up_full = (
        lax.all_gather(value_weight, "dp", axis=0, tiled=True),
        lax.all_gather(output_weight, "dp", axis=0, tiled=True),
        lax.all_gather(adapter_down_factor, "dp", axis=0, tiled=True),
        lax.all_gather(adapter_up_factor, "dp", axis=0, tiled=True),
    )
    depth_all, slot_all = (
        lax.all_gather(depths, "seq", axis=0, tiled=True),
        lax.all_gather(packed_slot_index, "seq", axis=0, tiled=True),
    )
    active_all = depth_all >= 2
    dest_all = jnp.where(active_all, slot_all // act_rows, -1)
    pos_all = jnp.where(active_all, slot_all % act_rows, 0)
    mine = active_all & (dest_all == own_index)
    active = depths >= 2
    zero_row = jnp.zeros((), jnp.bfloat16)
    rows_all = lax.all_gather(hidden, "seq", axis=0, tiled=True)
    source = (
        jnp.zeros((act_rows,), jnp.int32)
        .at[jnp.where(mine, pos_all, act_rows)]
        .set(jnp.arange(seq_count * tok_count, dtype=jnp.int32), mode="drop")
    )
    packed = jnp.take(rows_all, source, axis=0)
    looped, gradient_rows, down_factor_gradient, up_factor_gradient = layer_forward(
        packed,
        cotangent,
        value_full,
        out_full,
        down_full,
        up_full,
        before_norm_gain,
        after_norm_gain,
    )
    grads_all = lax.all_gather(gradient_rows, "seq", axis=0, tiled=True)
    picked = jnp.take(grads_all, jnp.maximum(packed_slot_index, 0), axis=0)
    grad_hidden = jnp.where(active[:, None], picked, zero_row)
    grad_scale = 1.0 / math.sqrt(seq_count * act_rows * lax.axis_size("dp"))
    down_term = down_factor_gradient * grad_scale
    up_term = up_factor_gradient * grad_scale
    down_mid, up_mid = (
        lax.psum_scatter(
            down_term.astype(jnp.bfloat16), "seq", scatter_dimension=1, tiled=True
        ).astype(jnp.float32),
        lax.psum_scatter(
            up_term.astype(jnp.bfloat16), "seq", scatter_dimension=1, tiled=True
        ).astype(jnp.float32),
    )
    down_sum, up_sum = (
        lax.psum_scatter(down_mid, "dp", scatter_dimension=0, tiled=True),
        lax.psum_scatter(up_mid, "dp", scatter_dimension=0, tiled=True),
    )
    return (looped, grad_hidden, down_sum, up_sum)


MESH = pl.DeviceIdType.MESH
BF, F32 = jnp.bfloat16, jnp.float32
CAP = 64


def dot(left, right, left_axis=1, right_axis=0):
    return lax.dot_general(
        left, right, (((left_axis,), (right_axis,)), ((), ())), preferred_element_type=F32
    )


def fused_kernel(
    slot_ref, depth_ref, gain_b_ref, gain_a_ref, hidden_hbm, cot_hbm, wv_in, wo_in, dn_in, up_in,
    looped_hbm, gh_hbm, lora_out,
    wv, wo, dn, up, hid, cot, sendb, recvb, gsend, grecv, lsend, lrecv, zsend, zrecv,
    place, unplace, normed, low, proj, mixed, gv, gn, packed, looped,
    w_send, w_recv, s_send, s_recv, l_send, l_recv, g_send, g_recv, z_send, z_recv, loc,
):
    dp, seq = lax.axis_index("dp"), lax.axis_index("seq")
    n_dp, n_seq = 8, 4
    width = hid.shape[1]
    core, x, y = dp % 2, (dp // 2) % 2, dp // 4
    nbr_x, nbr_y, sib = dp + 2 - 4 * x, dp + 4 - 8 * y, dp + 1 - 2 * core
    diag = nbr_x + 4 - 8 * y
    to_sib = 1 - 2 * core
    partner = seq + 1 - 2 * (seq % 2)
    side = (core + seq) % 2
    turn_from = nbr_x + side * (nbr_y - nbr_x)
    turn_to = nbr_y + side * (nbr_x - nbr_y)

    local = [
        pltpu.make_async_copy(hidden_hbm, hid, loc.at[0]),
        pltpu.make_async_copy(cot_hbm, cot, loc.at[1]),
    ]
    arrays = [(dn_in, dn), (up_in, up), (wv_in, wv), (wo_in, wo)]
    for number, (shard, full) in enumerate(arrays):
        rows = shard.shape[0]
        local.append(
            pltpu.make_async_copy(
                shard, full.at[pl.ds(pl.multiple_of(dp * rows, 16), rows), :], loc.at[2 + number]
            )
        )
    for copy in local:
        copy.start()

    barrier = pltpu.get_barrier_semaphore()
    for k in range(1, n_dp):
        pl.semaphore_signal(barrier, inc=1, device_id=((dp + k) % n_dp, seq), device_id_type=MESH)
    for k in range(1, n_seq):
        pl.semaphore_signal(barrier, inc=1, device_id=(dp, (seq + k) % n_seq), device_id_type=MESH)

    tok = hid.shape[0]
    slots = slot_ref[...]
    act = depth_ref[...] >= 2
    dest = jnp.where(act, slots // 128, -1)
    where_to = lax.broadcasted_iota(jnp.int32, (8, tok), 0) == dest
    earlier = (
        lax.broadcasted_iota(jnp.int32, (tok, tok), 0)
        < lax.broadcasted_iota(jnp.int32, (tok, tok), 1)
    ).astype(F32).astype(BF)
    counts = dot(where_to.astype(F32).astype(BF), earlier)
    rank = jnp.sum(jnp.where(where_to, counts, 0.0), axis=0, keepdims=True)
    row_of = jnp.where(act, dest.astype(F32) * CAP + rank, -1.0)
    picked = (lax.broadcasted_iota(jnp.int32, (n_seq * CAP, tok), 0).astype(F32) == row_of).astype(F32)
    place[...] = picked.astype(BF)
    position = jnp.where(act, slots - dest * 128 + 1, 0).astype(F32)
    pos_col = jnp.sum(picked * position, axis=1, keepdims=True) - 1.0
    sendb[:, width:] = jnp.broadcast_to(pos_col, (n_seq * CAP, 128)).astype(BF)

    pl.semaphore_wait(barrier, n_dp - 1 + n_seq - 1)

    def region(a, owner, half):
        shard, full = arrays[a]
        rows = shard.shape[0]
        if half is None:
            return full.at[pl.ds(pl.multiple_of(owner * rows, 16), rows), :]
        part = rows // 2
        return full.at[pl.ds(pl.multiple_of(owner * rows + half * part, 16), part), :]

    def piece(a, number, owner, half, target, from_input=False, at_seq=None):
        dst = region(a, owner, half)
        if from_input:
            shard = arrays[a][0]
            part = shard.shape[0] // 2
            source = shard if half is None else shard.at[pl.ds(half * part, part), :]
        else:
            source = dst
        return pltpu.make_async_remote_copy(
            src_ref=source, dst_ref=dst, send_sem=w_send.at[a * 13 + number],
            recv_sem=w_recv.at[a * 13 + number],
            device_id=(target, seq if at_seq is None else at_seq), device_id_type=MESH,
        )

    pending = []

    def send(*args, **kw):
        copy = piece(*args, **kw)
        copy.start()
        pending.append(copy)

    def got(a, number, owner, half):
        piece(a, number, owner, half, sib).wait_recv()

    def own_first(a):
        send(a, 0, dp, 0, nbr_x, from_input=True)
        send(a, 3, dp, 1, nbr_y, from_input=True)
        send(a, 6, dp, None, sib, from_input=True)

    def own_second(a):
        send(a, 1, dp, 1, nbr_x, from_input=True)
        send(a, 2, dp, 0, nbr_y, from_input=True)

    def forward_first(a):
        got(a, 0, nbr_x, 0)
        got(a, 3, nbr_y, 1)
        send(a, 4, turn_from, side, turn_to)
        send(a, 7, nbr_x, 0, sib)
        send(a, 8, nbr_y, 1, sib)

    def forward_second(a):
        got(a, 1, nbr_x, 1)
        send(a, 9, nbr_x, 1, sib)
        got(a, 2, nbr_y, 0)
        send(a, 10, nbr_y, 0, sib)

    def forward_diag(a):
        got(a, 4, diag, side)
        send(a, 5, diag, side, dp, at_seq=partner)
        send(a, 11, diag, side, sib)

    def forward_partner(a):
        got(a, 5, diag, 1 - side)
        send(a, 12, diag, 1 - side, sib)

    def finish(a):
        got(a, 6, sib, None)
        got(a, 7, nbr_x + to_sib, 0)
        got(a, 8, nbr_y + to_sib, 1)
        got(a, 9, nbr_x + to_sib, 1)
        got(a, 10, nbr_y + to_sib, 0)
        got(a, 11, diag + to_sib, 1 - side)
        got(a, 12, diag + to_sib, side)

    for a in (0, 1, 2, 3):
        own_first(a)

    def block(owner, rows):
        return pl.ds(pl.multiple_of(owner * rows, 16), rows)

    def exchange(src_buf, dst_buf, sends, recvs, k):
        target = (seq + k) % n_seq
        return pltpu.make_async_remote_copy(
            src_ref=src_buf.at[block(target, CAP), :], dst_ref=dst_buf.at[block(seq, CAP), :],
            send_sem=sends.at[k], recv_sem=recvs.at[k], device_id=(dp, target), device_id_type=MESH,
        )

    def arrival(src_buf, dst_buf, sends, recvs, k):
        origin = (seq + n_seq - k) % n_seq
        here = dst_buf.at[block(origin, CAP), :]
        pltpu.make_async_remote_copy(
            src_ref=here, dst_ref=here, send_sem=sends.at[k], recv_sem=recvs.at[k],
            device_id=(dp, origin), device_id_type=MESH,
        ).wait_recv()

    local[0].wait()
    sendb[:, :width] = dot(place[...], hid[...]).astype(BF)
    for k in (2, 1, 3):
        copy = exchange(sendb, recvb, s_send, s_recv, k)
        copy.start()
        pending.append(copy)
    recvb[block(seq, CAP), :] = sendb[block(seq, CAP), :]

    for a in (0, 1, 2, 3):
        forward_first(a)
    for a in (0, 1, 2):
        own_second(a)
    for a in (0, 1, 2, 3):
        forward_diag(a)
    for a in (0, 1, 2):
        forward_second(a)
    own_second(3)
    for a in (0, 1, 2, 3):
        forward_partner(a)

    for k in (1, 2, 3):
        arrival(sendb, recvb, s_send, s_recv, k)
    lanes = lax.broadcasted_iota(jnp.int32, (n_seq * CAP, 128), 1).astype(F32)
    unplace[...] = (recvb[:, width:].astype(F32) == lanes).astype(F32).astype(BF)
    x_float = dot(unplace[...], recvb[:, :width], 0, 0)
    packed[...] = x_float
    inv_pre = lax.rsqrt(jnp.mean(x_float * x_float, axis=-1, keepdims=True) + epsilon)
    normed[...] = (x_float * inv_pre * gain_b_ref[...].reshape(1, width)).astype(BF)

    for copy in local[1:]:
        copy.wait()
    for a in (0, 1, 2):
        finish(a)

    low[...] = dot(normed[...], dn[...]).astype(BF)

    tile = 256

    @pl.loop(0, proj.shape[1] // tile)
    def _(n):
        at = pl.ds(pl.multiple_of(n * tile, tile), tile)
        proj[:, at] = (
            dot(normed[...], wv[:, at]) + dot(low[...], up[at, :], 1, 1)
        ).astype(BF)

    forward_second(3)
    finish(3)

    @pl.loop(0, width // tile)
    def _(n):
        at = pl.ds(pl.multiple_of(n * tile, tile), tile)
        mixed[:, at] = dot(proj[...], wo[:, at])

    m = mixed[...]
    inv_post = lax.rsqrt(jnp.mean(m * m, axis=-1, keepdims=True) + epsilon)
    shaped = m * inv_post
    gain_a = gain_a_ref[...].reshape(1, width)
    looped[...] = (packed[...] + shaped * gain_a).astype(BF)
    loop_out = pltpu.make_async_copy(looped, looped_hbm, loc.at[6])
    loop_out.start()
    grad_shaped = cot[...].astype(F32) * gain_a
    mixed[...] = inv_post * (
        grad_shaped - shaped * jnp.mean(grad_shaped * shaped, axis=-1, keepdims=True)
    )

    @pl.loop(0, gv.shape[1] // tile)
    def _(n):
        at = pl.ds(pl.multiple_of(n * tile, tile), tile)
        gv[:, at] = dot(mixed[...].astype(BF), wo[at, :], 1, 1).astype(BF)

    grad_low = dot(gv[...], up[...]).astype(BF)

    @pl.loop(0, width // tile)
    def _(n):
        at = pl.ds(pl.multiple_of(n * tile, tile), tile)
        gn[:, at] = dot(gv[...], wv[at, :], 1, 1) + dot(grad_low, dn[at, :], 1, 1)

    x_float = packed[...]
    inv_pre = lax.rsqrt(jnp.mean(x_float * x_float, axis=-1, keepdims=True) + epsilon)
    whitened = x_float * inv_pre
    grad_white = gn[...] * gain_b_ref[...].reshape(1, width)
    grad_packed = (
        cot[...].astype(F32)
        + inv_pre
        * (grad_white - whitened * jnp.mean(grad_white * whitened, axis=-1, keepdims=True))
    ).astype(BF)
    gsend[...] = dot(unplace[...], grad_packed).astype(BF)
    for k in (2, 1, 3):
        copy = exchange(gsend, grecv, g_send, g_recv, k)
        copy.start()
        pending.append(copy)
    grecv[block(seq, CAP), :] = gsend[block(seq, CAP), :]

    down_rows, up_rows = dn_in.shape[0], up_in.shape[0]
    down_term = dot(normed[...], grad_low, 0, 0).astype(BF)
    up_term = dot(gv[...], low[...], 0, 0).astype(BF)
    for owner in range(n_dp):
        lsend[owner, :down_rows, :] = down_term[owner * down_rows : (owner + 1) * down_rows, :]
        lsend[owner, down_rows:, :] = up_term[owner * up_rows : (owner + 1) * up_rows, :]
    for k in range(1, n_dp):
        target = (dp + k) % n_dp
        copy = pltpu.make_async_remote_copy(
            src_ref=lsend.at[target], dst_ref=lrecv.at[dp], send_sem=l_send.at[k],
            recv_sem=l_recv.at[k], device_id=(target, seq), device_id_type=MESH,
        )
        copy.start()
        pending.append(copy)
    lrecv[dp] = lsend[dp]

    for k in range(1, n_dp):
        origin = (dp + n_dp - k) % n_dp
        here = lrecv.at[origin]
        pltpu.make_async_remote_copy(
            src_ref=here, dst_ref=here, send_sem=l_send.at[k], recv_sem=l_recv.at[k],
            device_id=(origin, seq), device_id_type=MESH,
        ).wait_recv()
    total = lrecv[0].astype(F32)
    for owner in range(1, n_dp):
        total += lrecv[owner].astype(F32)
    lead = total.shape[0]
    pad = zsend.shape[1] - lead
    total = jnp.concatenate([total, jnp.zeros((pad, total.shape[1]), F32)], axis=0)
    zsend[...] = total.T.astype(BF)
    cols = lora_out.shape[0]
    for k in range(1, n_seq):
        target = (seq + k) % n_seq
        copy = pltpu.make_async_remote_copy(
            src_ref=zsend.at[pl.ds(pl.multiple_of(target * cols, 16), cols), :],
            dst_ref=zrecv.at[seq], send_sem=z_send.at[k], recv_sem=z_recv.at[k],
            device_id=(dp, target), device_id_type=MESH,
        )
        copy.start()
        pending.append(copy)
    zrecv[seq] = zsend[pl.ds(pl.multiple_of(seq * cols, 16), cols), :]

    for k in (1, 2, 3):
        arrival(gsend, grecv, g_send, g_recv, k)
    hid[...] = dot(place[...], grecv[...], 0, 0).astype(BF)
    grad_out = pltpu.make_async_copy(hid, gh_hbm, loc.at[7])
    grad_out.start()

    for k in range(1, n_seq):
        origin = (seq + n_seq - k) % n_seq
        here = zrecv.at[origin]
        pltpu.make_async_remote_copy(
            src_ref=here, dst_ref=here, send_sem=z_send.at[k], recv_sem=z_recv.at[k],
            device_id=(dp, origin), device_id_type=MESH,
        ).wait_recv()
    grad_scale = 1.0 / math.sqrt(n_seq * cot.shape[0] * n_dp)
    z = [zrecv[owner].astype(F32) for owner in range(n_seq)]
    lora_out[...] = ((z[0] + z[1]) + (z[2] + z[3])) * grad_scale
    for copy in pending:
        copy.wait_send()
    loop_out.wait()
    grad_out.wait()


def fused_body(
    hidden, depths, packed_slot_index, value_weight, output_weight, adapter_down_factor,
    adapter_up_factor, before_norm_gain, after_norm_gain, cotangent,
):
    tok, width = hidden.shape
    act = cotangent.shape[0]
    n_dp, n_seq = lax.axis_size("dp"), lax.axis_size("seq")
    v_rows, value_width = value_weight.shape
    o_rows = output_weight.shape[0]
    rank = adapter_up_factor.shape[1]
    u_rows = adapter_up_factor.shape[0]
    cols = rank // n_seq
    lead = v_rows + u_rows
    lead_pad = -(-lead // 128) * 128
    vm, hbm = pl.BlockSpec(memory_space=pltpu.VMEM), pl.BlockSpec(memory_space=pltpu.HBM)
    dma = pltpu.SemaphoreType.DMA
    rows = n_seq * CAP
    looped, grad_hidden, lora = pl.pallas_call(
        fused_kernel,
        out_shape=(
            jax.ShapeDtypeStruct((act, width), BF),
            jax.ShapeDtypeStruct((tok, width), BF),
            jax.ShapeDtypeStruct((cols, lead_pad), F32),
        ),
        in_specs=[vm] * 4 + [hbm] * 6,
        out_specs=(hbm, hbm, vm),
        scratch_shapes=[
            pltpu.VMEM((v_rows * n_dp, value_width), BF),
            pltpu.VMEM((o_rows * n_dp, width), BF),
            pltpu.VMEM((v_rows * n_dp, rank), BF),
            pltpu.VMEM((u_rows * n_dp, rank), BF),
            pltpu.VMEM((tok, width), BF),
            pltpu.VMEM((act, width), BF),
            pltpu.VMEM((rows, width + 128), BF),
            pltpu.VMEM((rows, width + 128), BF),
            pltpu.VMEM((rows, width), BF),
            pltpu.VMEM((rows, width), BF),
            pltpu.VMEM((n_dp, lead, rank), BF),
            pltpu.VMEM((n_dp, lead, rank), BF),
            pltpu.VMEM((rank, lead_pad), BF),
            pltpu.VMEM((n_seq, cols, lead_pad), BF),
            pltpu.VMEM((rows, tok), BF),
            pltpu.VMEM((rows, 128), BF),
            pltpu.VMEM((act, width), BF),
            pltpu.VMEM((act, rank), BF),
            pltpu.VMEM((act, value_width), BF),
            pltpu.VMEM((act, width), F32),
            pltpu.VMEM((act, value_width), BF),
            pltpu.VMEM((act, width), F32),
            pltpu.VMEM((act, width), F32),
            pltpu.VMEM((act, width), BF),
            dma((52,)), dma((52,)), dma((4,)), dma((4,)), dma((8,)), dma((8,)),
            dma((4,)), dma((4,)), dma((4,)), dma((4,)), dma((8,)),
        ],
        compiler_params=pltpu.CompilerParams(
            collective_id=0, has_side_effects=True, vmem_limit_bytes=62 << 20
        ),
    )(
        packed_slot_index.reshape(1, tok),
        depths.reshape(1, tok),
        before_norm_gain,
        after_norm_gain,
        hidden,
        cotangent,
        value_weight,
        output_weight,
        adapter_down_factor,
        adapter_up_factor,
    )
    return looped, grad_hidden, lora[:, :v_rows].T, lora[:, v_rows:lead].T


def body(*arrays):
    fits = (
        lax.axis_size("dp") == 8
        and lax.axis_size("seq") == 4
        and arrays[0].shape[0] == 4 * CAP
        and arrays[9].shape[0] == 128
        and arrays[0].shape[1] % 256 == 0
        and arrays[3].shape[1] % 256 == 0
        and all(arrays[i].shape[0] % 32 == 0 for i in (3, 4, 5, 6))
        and arrays[6].shape[1] == 128
    )
    return (fused_body if fits else general_body)(*arrays)


def solution(mesh):
    placed = (
        P(("dp", "seq"), None),
        P(("dp", "seq")),
        P(("dp", "seq")),
        P("dp", None),
        P("dp", None),
        P("dp", None),
        P("dp", None),
        P(),
        P(),
        P(("dp", "seq"), None),
    )
    return jax.shard_map(
        body,
        mesh=mesh,
        in_specs=placed,
        out_specs=(P(("dp", "seq"), None), P(("dp", "seq"), None), P("dp", "seq"), P("dp", "seq")),
        check_vma=False,
    )
```

```python
import functools
import math

import jax
import jax.numpy as jnp
from jax import lax
from jax.experimental import pallas as pl
from jax.experimental.pallas import tpu as pltpu
from jax.sharding import PartitionSpec as P

epsilon = 1e-06


def contract_final_axis(left, right):
    return lax.dot_general(
        left, right, (((1,), (1,)), ((), ())), preferred_element_type=jnp.float32
    )


def contract_first(left, right):
    return lax.dot_general(
        left, right, (((0,), (0,)), ((), ())), preferred_element_type=jnp.float32
    )


def layer_forward(
    input_rows,
    cotangent_rows,
    value_weight,
    output_weight,
    adapter_down_factor,
    adapter_up_factor,
    before_norm_gain,
    after_norm_gain,
):
    x_float = input_rows.astype(jnp.float32)
    inv_pre = lax.rsqrt(jnp.mean(x_float * x_float, axis=-1, keepdims=True) + epsilon)
    whitened = x_float * inv_pre
    normalized_rows = (whitened * before_norm_gain).astype(jnp.bfloat16)
    rank_reduced = jnp.dot(
        normalized_rows, adapter_down_factor, preferred_element_type=jnp.float32
    ).astype(jnp.bfloat16)
    projected_rows = (
        jnp.dot(normalized_rows, value_weight, preferred_element_type=jnp.float32)
        + contract_final_axis(rank_reduced, adapter_up_factor)
    ).astype(jnp.bfloat16)
    mixed_out = jnp.dot(projected_rows, output_weight, preferred_element_type=jnp.float32)
    inv_post = lax.rsqrt(jnp.mean(mixed_out * mixed_out, axis=-1, keepdims=True) + epsilon)
    shaped = mixed_out * inv_post
    looped = (x_float + shaped * after_norm_gain).astype(jnp.bfloat16)
    cot_float = cotangent_rows.astype(jnp.float32)
    grad_shaped = cot_float * after_norm_gain
    grad_mixed = (
        inv_post * (grad_shaped - shaped * jnp.mean(grad_shaped * shaped, axis=-1, keepdims=True))
    ).astype(jnp.bfloat16)
    value_gradient = contract_final_axis(grad_mixed, output_weight).astype(jnp.bfloat16)
    low_rank_gradient = jnp.dot(
        value_gradient, adapter_up_factor, preferred_element_type=jnp.float32
    ).astype(jnp.bfloat16)
    normalized_gradient = contract_final_axis(value_gradient, value_weight) + contract_final_axis(
        low_rank_gradient, adapter_down_factor
    )
    grad_white = normalized_gradient * before_norm_gain
    gradient_rows = (
        cot_float
        + inv_pre
        * (grad_white - whitened * jnp.mean(grad_white * whitened, axis=-1, keepdims=True))
    ).astype(jnp.bfloat16)
    down_factor_gradient = contract_first(normalized_rows, low_rank_gradient)
    up_factor_gradient = contract_first(value_gradient, rank_reduced)
    return (looped, gradient_rows, down_factor_gradient, up_factor_gradient)


def general_body(
    hidden,
    depths,
    packed_slot_index,
    value_weight,
    output_weight,
    adapter_down_factor,
    adapter_up_factor,
    before_norm_gain,
    after_norm_gain,
    cotangent,
):
    seq_count = lax.axis_size("seq")
    own_index = lax.axis_index("seq")
    tok_count = hidden.shape[0]
    act_rows = cotangent.shape[0]
    value_full, out_full, down_full, up_full = (
        lax.all_gather(value_weight, "dp", axis=0, tiled=True),
        lax.all_gather(output_weight, "dp", axis=0, tiled=True),
        lax.all_gather(adapter_down_factor, "dp", axis=0, tiled=True),
        lax.all_gather(adapter_up_factor, "dp", axis=0, tiled=True),
    )
    depth_all, slot_all = (
        lax.all_gather(depths, "seq", axis=0, tiled=True),
        lax.all_gather(packed_slot_index, "seq", axis=0, tiled=True),
    )
    active_all = depth_all >= 2
    dest_all = jnp.where(active_all, slot_all // act_rows, -1)
    pos_all = jnp.where(active_all, slot_all % act_rows, 0)
    mine = active_all & (dest_all == own_index)
    active = depths >= 2
    zero_row = jnp.zeros((), jnp.bfloat16)
    rows_all = lax.all_gather(hidden, "seq", axis=0, tiled=True)
    source = (
        jnp.zeros((act_rows,), jnp.int32)
        .at[jnp.where(mine, pos_all, act_rows)]
        .set(jnp.arange(seq_count * tok_count, dtype=jnp.int32), mode="drop")
    )
    packed = jnp.take(rows_all, source, axis=0)
    looped, gradient_rows, down_factor_gradient, up_factor_gradient = layer_forward(
        packed,
        cotangent,
        value_full,
        out_full,
        down_full,
        up_full,
        before_norm_gain,
        after_norm_gain,
    )
    grads_all = lax.all_gather(gradient_rows, "seq", axis=0, tiled=True)
    picked = jnp.take(grads_all, jnp.maximum(packed_slot_index, 0), axis=0)
    grad_hidden = jnp.where(active[:, None], picked, zero_row)
    grad_scale = 1.0 / math.sqrt(seq_count * act_rows * lax.axis_size("dp"))
    down_term = down_factor_gradient * grad_scale
    up_term = up_factor_gradient * grad_scale
    down_mid, up_mid = (
        lax.psum_scatter(
            down_term.astype(jnp.bfloat16), "seq", scatter_dimension=1, tiled=True
        ).astype(jnp.float32),
        lax.psum_scatter(
            up_term.astype(jnp.bfloat16), "seq", scatter_dimension=1, tiled=True
        ).astype(jnp.float32),
    )
    down_sum, up_sum = (
        lax.psum_scatter(down_mid, "dp", scatter_dimension=0, tiled=True),
        lax.psum_scatter(up_mid, "dp", scatter_dimension=0, tiled=True),
    )
    return (looped, grad_hidden, down_sum, up_sum)


MESH = pl.DeviceIdType.MESH
BF, F32 = jnp.bfloat16, jnp.float32
CAP = 64


def dot(left, right, left_axis=1, right_axis=0):
    return lax.dot_general(
        left, right, (((left_axis,), (right_axis,)), ((), ())), preferred_element_type=F32
    )


def fused_kernel(
    slot_ref, depth_ref, gain_b_ref, gain_a_ref, hidden_hbm, cot_hbm, wv_in, wo_in, dn_in, up_in,
    looped_hbm, gh_hbm, lora_out,
    wv, wo, dn, up, hid, cot, sendb, recvb, gsend, grecv, lsend, lrecv, zsend, zrecv,
    place, unplace, normed, low, proj, mixed, gv, gn, packed, looped,
    w_send, w_recv, s_send, s_recv, l_send, l_recv, g_send, g_recv, z_send, z_recv, loc,
):
    dp, seq = lax.axis_index("dp"), lax.axis_index("seq")
    n_dp, n_seq = 8, 4
    width = hid.shape[1]
    core, x, y = dp % 2, (dp // 2) % 2, dp // 4
    nbr_x, nbr_y, sib = dp + 2 - 4 * x, dp + 4 - 8 * y, dp + 1 - 2 * core
    diag = nbr_x + 4 - 8 * y
    to_sib = 1 - 2 * core
    partner = seq + 1 - 2 * (seq % 2)
    side = (core + seq) % 2
    turn_from = nbr_x + side * (nbr_y - nbr_x)
    turn_to = nbr_y + side * (nbr_x - nbr_y)

    local = [
        pltpu.make_async_copy(hidden_hbm, hid, loc.at[0]),
        pltpu.make_async_copy(cot_hbm, cot, loc.at[1]),
    ]
    arrays = [(dn_in, dn), (up_in, up), (wv_in, wv), (wo_in, wo)]
    for number, (shard, full) in enumerate(arrays):
        rows = shard.shape[0]
        local.append(
            pltpu.make_async_copy(
                shard, full.at[pl.ds(pl.multiple_of(dp * rows, 16), rows), :], loc.at[2 + number]
            )
        )
    for copy in local:
        copy.start()

    barrier = pltpu.get_barrier_semaphore()
    for k in range(1, n_dp):
        pl.semaphore_signal(barrier, inc=1, device_id=((dp + k) % n_dp, seq), device_id_type=MESH)
    for k in range(1, n_seq):
        pl.semaphore_signal(barrier, inc=1, device_id=(dp, (seq + k) % n_seq), device_id_type=MESH)

    tok = hid.shape[0]
    slots = slot_ref[...]
    act = depth_ref[...] >= 2
    dest = jnp.where(act, slots // 128, -1)
    where_to = lax.broadcasted_iota(jnp.int32, (8, tok), 0) == dest
    earlier = (
        lax.broadcasted_iota(jnp.int32, (tok, tok), 0)
        < lax.broadcasted_iota(jnp.int32, (tok, tok), 1)
    ).astype(F32).astype(BF)
    counts = dot(where_to.astype(F32).astype(BF), earlier)
    rank = jnp.sum(jnp.where(where_to, counts, 0.0), axis=0, keepdims=True)
    row_of = jnp.where(act, dest.astype(F32) * CAP + rank, -1.0)
    picked = (lax.broadcasted_iota(jnp.int32, (n_seq * CAP, tok), 0).astype(F32) == row_of).astype(F32)
    place[...] = picked.astype(BF)
    position = jnp.where(act, slots - dest * 128 + 1, 0).astype(F32)
    pos_col = jnp.sum(picked * position, axis=1, keepdims=True) - 1.0
    sendb[:, width:] = jnp.broadcast_to(pos_col, (n_seq * CAP, 128)).astype(BF)

    pl.semaphore_wait(barrier, n_dp - 1 + n_seq - 1)

    def region(a, owner, half):
        shard, full = arrays[a]
        rows = shard.shape[0]
        if half is None:
            return full.at[pl.ds(pl.multiple_of(owner * rows, 16), rows), :]
        part = rows // 2
        return full.at[pl.ds(pl.multiple_of(owner * rows + half * part, 16), part), :]

    def piece(a, number, owner, half, target, from_input=False, at_seq=None):
        dst = region(a, owner, half)
        if from_input:
            shard = arrays[a][0]
            part = shard.shape[0] // 2
            source = shard if half is None else shard.at[pl.ds(half * part, part), :]
        else:
            source = dst
        return pltpu.make_async_remote_copy(
            src_ref=source, dst_ref=dst, send_sem=w_send.at[a * 13 + number],
            recv_sem=w_recv.at[a * 13 + number],
            device_id=(target, seq if at_seq is None else at_seq), device_id_type=MESH,
        )

    pending = []

    def send(*args, **kw):
        copy = piece(*args, **kw)
        copy.start()
        pending.append(copy)

    def got(a, number, owner, half):
        piece(a, number, owner, half, sib).wait_recv()

    def own_first(a):
        send(a, 0, dp, 0, nbr_x, from_input=True)
        send(a, 3, dp, 1, nbr_y, from_input=True)
        send(a, 6, dp, None, sib, from_input=True)

    def own_second(a):
        send(a, 1, dp, 1, nbr_x, from_input=True)
        send(a, 2, dp, 0, nbr_y, from_input=True)

    def forward_first(a):
        got(a, 0, nbr_x, 0)
        got(a, 3, nbr_y, 1)
        send(a, 4, turn_from, side, turn_to)
        send(a, 7, nbr_x, 0, sib)
        send(a, 8, nbr_y, 1, sib)

    def forward_second(a):
        got(a, 1, nbr_x, 1)
        send(a, 9, nbr_x, 1, sib)
        got(a, 2, nbr_y, 0)
        send(a, 10, nbr_y, 0, sib)

    def forward_diag(a):
        got(a, 4, diag, side)
        send(a, 5, diag, side, dp, at_seq=partner)
        send(a, 11, diag, side, sib)

    def forward_partner(a):
        got(a, 5, diag, 1 - side)
        send(a, 12, diag, 1 - side, sib)

    def finish(a):
        got(a, 6, sib, None)
        got(a, 7, nbr_x + to_sib, 0)
        got(a, 8, nbr_y + to_sib, 1)
        got(a, 9, nbr_x + to_sib, 1)
        got(a, 10, nbr_y + to_sib, 0)
        got(a, 11, diag + to_sib, 1 - side)
        got(a, 12, diag + to_sib, side)

    for a in (0, 1, 2, 3):
        own_first(a)

    def block(owner, rows):
        return pl.ds(pl.multiple_of(owner * rows, 16), rows)

    def exchange(src_buf, dst_buf, sends, recvs, k):
        target = (seq + k) % n_seq
        return pltpu.make_async_remote_copy(
            src_ref=src_buf.at[block(target, CAP), :], dst_ref=dst_buf.at[block(seq, CAP), :],
            send_sem=sends.at[k], recv_sem=recvs.at[k], device_id=(dp, target), device_id_type=MESH,
        )

    def arrival(src_buf, dst_buf, sends, recvs, k):
        origin = (seq + n_seq - k) % n_seq
        here = dst_buf.at[block(origin, CAP), :]
        pltpu.make_async_remote_copy(
            src_ref=here, dst_ref=here, send_sem=sends.at[k], recv_sem=recvs.at[k],
            device_id=(dp, origin), device_id_type=MESH,
        ).wait_recv()

    local[0].wait()
    sendb[:, :width] = dot(place[...], hid[...]).astype(BF)
    for k in (2, 1, 3):
        copy = exchange(sendb, recvb, s_send, s_recv, k)
        copy.start()
        pending.append(copy)
    recvb[block(seq, CAP), :] = sendb[block(seq, CAP), :]

    for a in (0, 1, 2, 3):
        forward_first(a)
    for a in (0, 1, 2):
        own_second(a)
    for a in (0, 1, 2, 3):
        forward_diag(a)
    for a in (0, 1, 2):
        forward_second(a)
    own_second(3)
    for a in (0, 1, 2, 3):
        forward_partner(a)

    for k in (1, 2, 3):
        arrival(sendb, recvb, s_send, s_recv, k)
    lanes = lax.broadcasted_iota(jnp.int32, (n_seq * CAP, 128), 1).astype(F32)
    unplace[...] = (recvb[:, width:].astype(F32) == lanes).astype(F32).astype(BF)
    x_float = dot(unplace[...], recvb[:, :width], 0, 0)
    packed[...] = x_float
    inv_pre = lax.rsqrt(jnp.mean(x_float * x_float, axis=-1, keepdims=True) + epsilon)
    normed[...] = (x_float * inv_pre * gain_b_ref[...].reshape(1, width)).astype(BF)

    for copy in local[1:]:
        copy.wait()
    for a in (0, 1, 2):
        finish(a)

    low[...] = dot(normed[...], dn[...]).astype(BF)

    tile = 256

    @pl.loop(0, proj.shape[1] // tile, unroll=True)
    def _(n):
        at = pl.ds(pl.multiple_of(n * tile, tile), tile)
        proj[:, at] = (
            dot(normed[...], wv[:, at]) + dot(low[...], up[at, :], 1, 1)
        ).astype(BF)

    forward_second(3)
    finish(3)

    @pl.loop(0, width // tile, unroll=True)
    def _(n):
        at = pl.ds(pl.multiple_of(n * tile, tile), tile)
        mixed[:, at] = dot(proj[...], wo[:, at])

    m = mixed[...]
    inv_post = lax.rsqrt(jnp.mean(m * m, axis=-1, keepdims=True) + epsilon)
    shaped = m * inv_post
    gain_a = gain_a_ref[...].reshape(1, width)
    looped[...] = (packed[...] + shaped * gain_a).astype(BF)
    loop_out = pltpu.make_async_copy(looped, looped_hbm, loc.at[6])
    loop_out.start()
    grad_shaped = cot[...].astype(F32) * gain_a
    mixed[...] = inv_post * (
        grad_shaped - shaped * jnp.mean(grad_shaped * shaped, axis=-1, keepdims=True)
    )

    @pl.loop(0, gv.shape[1] // tile, unroll=True)
    def _(n):
        at = pl.ds(pl.multiple_of(n * tile, tile), tile)
        gv[:, at] = dot(mixed[...].astype(BF), wo[at, :], 1, 1).astype(BF)

    grad_low = dot(gv[...], up[...]).astype(BF)

    @pl.loop(0, width // tile, unroll=True)
    def _(n):
        at = pl.ds(pl.multiple_of(n * tile, tile), tile)
        gn[:, at] = dot(gv[...], wv[at, :], 1, 1) + dot(grad_low, dn[at, :], 1, 1)

    x_float = packed[...]
    inv_pre = lax.rsqrt(jnp.mean(x_float * x_float, axis=-1, keepdims=True) + epsilon)
    whitened = x_float * inv_pre
    grad_white = gn[...] * gain_b_ref[...].reshape(1, width)
    grad_packed = (
        cot[...].astype(F32)
        + inv_pre
        * (grad_white - whitened * jnp.mean(grad_white * whitened, axis=-1, keepdims=True))
    ).astype(BF)
    gsend[...] = dot(unplace[...], grad_packed).astype(BF)
    for k in (2, 1, 3):
        copy = exchange(gsend, grecv, g_send, g_recv, k)
        copy.start()
        pending.append(copy)
    grecv[block(seq, CAP), :] = gsend[block(seq, CAP), :]

    down_rows, up_rows = dn_in.shape[0], up_in.shape[0]
    down_term = dot(normed[...], grad_low, 0, 0).astype(BF)
    up_term = dot(gv[...], low[...], 0, 0).astype(BF)
    for owner in range(n_dp):
        lsend[owner, :down_rows, :] = down_term[owner * down_rows : (owner + 1) * down_rows, :]
        lsend[owner, down_rows:, :] = up_term[owner * up_rows : (owner + 1) * up_rows, :]
    for k in range(1, n_dp):
        target = (dp + k) % n_dp
        copy = pltpu.make_async_remote_copy(
            src_ref=lsend.at[target], dst_ref=lrecv.at[dp], send_sem=l_send.at[k],
            recv_sem=l_recv.at[k], device_id=(target, seq), device_id_type=MESH,
        )
        copy.start()
        pending.append(copy)
    lrecv[dp] = lsend[dp]

    for k in range(1, n_dp):
        origin = (dp + n_dp - k) % n_dp
        here = lrecv.at[origin]
        pltpu.make_async_remote_copy(
            src_ref=here, dst_ref=here, send_sem=l_send.at[k], recv_sem=l_recv.at[k],
            device_id=(origin, seq), device_id_type=MESH,
        ).wait_recv()
    total = lrecv[0].astype(F32)
    for owner in range(1, n_dp):
        total += lrecv[owner].astype(F32)
    lead = total.shape[0]
    pad = zsend.shape[1] - lead
    total = jnp.concatenate([total, jnp.zeros((pad, total.shape[1]), F32)], axis=0)
    zsend[...] = total.T.astype(BF)
    cols = lora_out.shape[0]
    for k in range(1, n_seq):
        target = (seq + k) % n_seq
        copy = pltpu.make_async_remote_copy(
            src_ref=zsend.at[pl.ds(pl.multiple_of(target * cols, 16), cols), :],
            dst_ref=zrecv.at[seq], send_sem=z_send.at[k], recv_sem=z_recv.at[k],
            device_id=(dp, target), device_id_type=MESH,
        )
        copy.start()
        pending.append(copy)
    zrecv[seq] = zsend[pl.ds(pl.multiple_of(seq * cols, 16), cols), :]

    for k in (1, 2, 3):
        arrival(gsend, grecv, g_send, g_recv, k)
    hid[...] = dot(place[...], grecv[...], 0, 0).astype(BF)
    grad_out = pltpu.make_async_copy(hid, gh_hbm, loc.at[7])
    grad_out.start()

    for k in range(1, n_seq):
        origin = (seq + n_seq - k) % n_seq
        here = zrecv.at[origin]
        pltpu.make_async_remote_copy(
            src_ref=here, dst_ref=here, send_sem=z_send.at[k], recv_sem=z_recv.at[k],
            device_id=(dp, origin), device_id_type=MESH,
        ).wait_recv()
    grad_scale = 1.0 / math.sqrt(n_seq * cot.shape[0] * n_dp)
    z = [zrecv[owner].astype(F32) for owner in range(n_seq)]
    lora_out[...] = ((z[0] + z[1]) + (z[2] + z[3])) * grad_scale
    for copy in pending:
        copy.wait_send()
    loop_out.wait()
    grad_out.wait()


def fused_body(
    hidden, depths, packed_slot_index, value_weight, output_weight, adapter_down_factor,
    adapter_up_factor, before_norm_gain, after_norm_gain, cotangent,
):
    tok, width = hidden.shape
    act = cotangent.shape[0]
    n_dp, n_seq = lax.axis_size("dp"), lax.axis_size("seq")
    v_rows, value_width = value_weight.shape
    o_rows = output_weight.shape[0]
    rank = adapter_up_factor.shape[1]
    u_rows = adapter_up_factor.shape[0]
    cols = rank // n_seq
    lead = v_rows + u_rows
    lead_pad = -(-lead // 128) * 128
    vm, hbm = pl.BlockSpec(memory_space=pltpu.VMEM), pl.BlockSpec(memory_space=pltpu.HBM)
    dma = pltpu.SemaphoreType.DMA
    rows = n_seq * CAP
    looped, grad_hidden, lora = pl.pallas_call(
        fused_kernel,
        out_shape=(
            jax.ShapeDtypeStruct((act, width), BF),
            jax.ShapeDtypeStruct((tok, width), BF),
            jax.ShapeDtypeStruct((cols, lead_pad), F32),
        ),
        in_specs=[vm] * 4 + [hbm] * 6,
        out_specs=(hbm, hbm, vm),
        scratch_shapes=[
            pltpu.VMEM((v_rows * n_dp, value_width), BF),
            pltpu.VMEM((o_rows * n_dp, width), BF),
            pltpu.VMEM((v_rows * n_dp, rank), BF),
            pltpu.VMEM((u_rows * n_dp, rank), BF),
            pltpu.VMEM((tok, width), BF),
            pltpu.VMEM((act, width), BF),
            pltpu.VMEM((rows, width + 128), BF),
            pltpu.VMEM((rows, width + 128), BF),
            pltpu.VMEM((rows, width), BF),
            pltpu.VMEM((rows, width), BF),
            pltpu.VMEM((n_dp, lead, rank), BF),
            pltpu.VMEM((n_dp, lead, rank), BF),
            pltpu.VMEM((rank, lead_pad), BF),
            pltpu.VMEM((n_seq, cols, lead_pad), BF),
            pltpu.VMEM((rows, tok), BF),
            pltpu.VMEM((rows, 128), BF),
            pltpu.VMEM((act, width), BF),
            pltpu.VMEM((act, rank), BF),
            pltpu.VMEM((act, value_width), BF),
            pltpu.VMEM((act, width), F32),
            pltpu.VMEM((act, value_width), BF),
            pltpu.VMEM((act, width), F32),
            pltpu.VMEM((act, width), F32),
            pltpu.VMEM((act, width), BF),
            dma((52,)), dma((52,)), dma((4,)), dma((4,)), dma((8,)), dma((8,)),
            dma((4,)), dma((4,)), dma((4,)), dma((4,)), dma((8,)),
        ],
        compiler_params=pltpu.CompilerParams(
            collective_id=0, has_side_effects=True, vmem_limit_bytes=(64 << 20) - (400 << 10)
        ),
    )(
        packed_slot_index.reshape(1, tok),
        depths.reshape(1, tok),
        before_norm_gain,
        after_norm_gain,
        hidden,
        cotangent,
        value_weight,
        output_weight,
        adapter_down_factor,
        adapter_up_factor,
    )
    return looped, grad_hidden, lora[:, :v_rows].T, lora[:, v_rows:lead].T


def body(*arrays):
    fits = (
        lax.axis_size("dp") == 8
        and lax.axis_size("seq") == 4
        and arrays[0].shape[0] == 4 * CAP
        and arrays[9].shape[0] == 128
        and arrays[0].shape[1] % 256 == 0
        and arrays[3].shape[1] % 256 == 0
        and all(arrays[i].shape[0] % 32 == 0 for i in (3, 4, 5, 6))
        and arrays[6].shape[1] == 128
    )
    return (fused_body if fits else general_body)(*arrays)


def solution(mesh):
    placed = (
        P(("dp", "seq"), None),
        P(("dp", "seq")),
        P(("dp", "seq")),
        P("dp", None),
        P("dp", None),
        P("dp", None),
        P("dp", None),
        P(),
        P(),
        P(("dp", "seq"), None),
    )
    return jax.shard_map(
        body,
        mesh=mesh,
        in_specs=placed,
        out_specs=(P(("dp", "seq"), None), P(("dp", "seq"), None), P("dp", "seq"), P("dp", "seq")),
        check_vma=False,
    )
```
